512 devices in a mesh: grp: 16 (over y, x), ch: 32 (over z, core).
Axes of the slice: x: 4, y: 4, z: 16, core: 2. Of those that a mesh axis runs over, the one named last changes fastest.
Arguments:
- x_in: bfloat16 [65536, 8192], P(('grp', 'ch')), may hold values from -6 to 6
- bc_in: bfloat16 [65536, 256], P(('grp', 'ch')), may hold values from -6 to 6
- dt_in: bfloat16 [65536, 128], P(('grp', 'ch')), may hold values from -2 to 14
- dt_bias: float32 [128], replicated, may hold values from -3 to -1
- a_log: float32 [128], P('ch'), may hold values from -7.5 to 0
- skip_d: float32 [128], P('ch'), may hold values from 0.5 to 1.5
- conv_x: float32 [4, 8192], P(None, 'ch'), may hold values from -3 to 3
- conv_x_bias: float32 [8192], P('ch'), may hold values from -3 to 3
- conv_bc: float32 [4, 256], replicated, may hold values from -3 to 3
- conv_bc_bias: float32 [256], replicated, may hold values from -3 to 3
- norm_gain: float32 [8192], replicated, may hold values from 0.5 to 1.5
- lengths: int32 [256], replicated, may hold values from 64 to 256, as said below
- dest_group: int32 [256], replicated, may hold values from -1 to 15, as said below
- dest_slot: int32 [256], replicated, may hold values from -1 to 15, as said below
Outputs:
- mixer_out: bfloat16 [65536, 8192], P(('grp', 'ch'))
The draws below stay inside these ranges and needn't reach their ends.
Inputs may be any that keep to these rules, and one draw needn't show every extreme that they name: `dest_group`: -1 marks a dropped pair. From one group at most 2 surviving pairs go to any one group, and every group sends exactly 2 to some group; one group's pairs go to at most 8 groups. `dest_slot`: -1 exactly where dest_group is -1; no two surviving pairs share a destination group and slot. `lengths`: every group holds at least one pair of length 256.
All inputs are finite; a program needn't handle non-finite values.
Results may differ from the reference program's by a relative error of at most 0.0053.
Values may be sent and summed in bfloat16 or wider, within the bound.
No kernel may reach another device: no remote copies, remote signals or barrier semaphores. Data moves between devices by JAX's collectives and lax.ppermute only.
A program may use at most 64 MiB of HBM per device.

```python
import jax
import jax.numpy as jnp
from jax import lax

INNER = 8192
STATE = 128
CONV = 4
CAP = 2
HEADS = 128
PAIR_LEN = 256
PAIRS_GRP = 16
TOKEN_SLOTS = 65536
N_GRP = 16


def draw_dt_in(key, part):
    noise_key = jax.random.fold_in(key, 7101)
    spurt_random_key = jax.random.fold_in(key, 7102)
    backdrop_noise = jnp.clip(0.5 * jax.random.normal(noise_key, (TOKEN_SLOTS, HEADS), jnp.float32), -2.0, 2.0)
    token_spurts = (jax.random.randint(spurt_random_key, (TOKEN_SLOTS, 1), 0, 64) == 0).astype(jnp.float32)
    return (backdrop_noise + 12.0 * token_spurts).astype(jnp.bfloat16)


def draw_a_log(key, part):
    rate_key = jax.random.fold_in(key, 7401)
    return jax.random.uniform(rate_key, (HEADS,), jnp.float32, -6.0, 0.0)


def draw_lengths(key, part):
    length_random_key = jax.random.fold_in(key, 7301)
    full_key = jax.random.fold_in(key, 7302)
    drawn = jax.random.randint(length_random_key, (N_GRP, PAIRS_GRP), PAIR_LEN // 4, PAIR_LEN + 1)
    full_at = jax.random.randint(full_key, (N_GRP, 1), 0, PAIRS_GRP)
    columns = jnp.arange(PAIRS_GRP, dtype=jnp.int32)[None, :]
    return jnp.where(columns == full_at, PAIR_LEN, drawn).reshape(-1).astype(jnp.int32)


def route_tables(key):
    table_key = jax.random.fold_in(key, 7201)
    offset_key, order_key, slot_key, keep_key = jax.random.split(table_key, 4)
    fanout = PAIRS_GRP // CAP
    others = (jax.random.permutation(offset_key, N_GRP - 1) + 1).astype(jnp.int32)
    offsets_raw = jnp.concatenate([jnp.zeros((1,), jnp.int32), others[:fanout - 1]])
    offsets = ((offsets_raw + N_GRP // 2) % N_GRP).astype(jnp.int32)
    groups = jnp.arange(N_GRP, dtype=jnp.int32)

    def order_of(member):
        return jax.random.permutation(jax.random.fold_in(order_key, member), PAIRS_GRP).astype(jnp.int32)

    def slots_of(member):
        return jax.random.permutation(jax.random.fold_in(slot_key, member), PAIRS_GRP).astype(jnp.int32)
    orders = jax.vmap(order_of)(groups)
    slot_orders = jax.vmap(slots_of)(groups)
    blocks = orders // CAP
    within = orders % CAP
    targets = (groups[:, None] + offsets[blocks]) % N_GRP
    slots = slot_orders[targets, blocks * CAP + within]
    keeps = (jax.random.randint(keep_key, (N_GRP, PAIRS_GRP), 0, 4) > 0) | (blocks == 0)
    group_table = jnp.where(keeps, targets, -1).reshape(-1).astype(jnp.int32)
    slot_table = jnp.where(keeps, slots, -1).reshape(-1).astype(jnp.int32)
    return (group_table, slot_table)


def draw_dest_group(key, part):
    return route_tables(key)[0]


def draw_dest_slot(key, part):
    return route_tables(key)[1]


def level_of(key, extent, cuts, least, largest):
    def one(axis_at, blocks):
        heights = jax.random.uniform(jax.random.fold_in(jax.random.fold_in(key, 6), axis_at), (blocks,), jnp.float32, least / len(cuts), largest / len(cuts))
        return jnp.repeat(jnp.exp(heights), extent[axis_at] // blocks).reshape((-1,) + (1,) * (len(extent) - axis_at - 1))

    gain = one(*cuts[0])
    for cut in cuts[1:]:
        gain = gain * one(*cut)
    return gain


def scatter_about(rng, extent, spread, reach, cuts=(), kind=jnp.bfloat16):
    loudness = level_of(rng, extent, cuts, -0.22, 0.18) if cuts else 1.0
    values = jax.random.normal(rng, extent, jnp.float32) * spread * loudness
    return jnp.minimum(jnp.maximum(values, -reach), reach).astype(kind)


def setup_inputs(seed: int = 0) -> dict:
    key_list = jax.random.split(jax.random.key(seed), 15)
    return {
        "x_in": scatter_about(key_list[0], (TOKEN_SLOTS, INNER), 1.0, 6.0, ((0, 512),)),
        "bc_in": scatter_about(key_list[1], (TOKEN_SLOTS, 2 * STATE), 1.0, 6.0, ((0, 512),)),
        "dt_in": draw_dt_in(jax.random.fold_in(key_list[14], 71), 0),
        "dt_bias": jnp.clip(jax.random.uniform(key_list[3], (HEADS,), jnp.float32, -3.0, -1.0), -3.0, -1.0),
        "a_log": draw_a_log(jax.random.fold_in(key_list[14], 71), 0),
        "skip_d": jnp.clip(0.5 + 1.0 * jax.random.uniform(key_list[5], (HEADS,), jnp.float32) ** level_of(key_list[5], (HEADS,), ((0, 32),), -0.2, 0.2), 0.5, 1.5),
        "conv_x": scatter_about(key_list[6], (CONV, INNER), CONV ** -0.5, 3.0, ((1, 32),), jnp.float32),
        "conv_x_bias": scatter_about(key_list[7], (INNER,), 0.5, 3.0, ((0, 32),), jnp.float32),
        "conv_bc": scatter_about(key_list[8], (CONV, 2 * STATE), CONV ** -0.5, 3.0, (), jnp.float32),
        "conv_bc_bias": scatter_about(key_list[9], (2 * STATE,), 0.5, 3.0, (), jnp.float32),
        "norm_gain": jnp.clip(1.0 + 0.1 * jax.random.normal(key_list[10], (INNER,), jnp.float32), 0.5, 1.5),
        "lengths": draw_lengths(jax.random.fold_in(key_list[14], 71), 0),
        "dest_group": draw_dest_group(jax.random.fold_in(key_list[14], 71), 0),
        "dest_slot": draw_dest_slot(jax.random.fold_in(key_list[14], 71), 0),
    }


def conv_silu(values, taps, bias):
    tap_count = taps.shape[0]
    length = values.shape[0]
    padded = jnp.concatenate([jnp.zeros((tap_count - 1, values.shape[1]), jnp.float32), values], axis=0)
    total = jnp.zeros_like(values) + bias[None, :]
    for offset in range(tap_count):
        total = total + taps[offset][None, :] * padded[offset:offset + length]
    return jax.nn.silu(total)

def mix_pair(x_pair, bc_pair, step_pair, conv_x, conv_x_bias, conv_bc, conv_bc_bias, decay_rate, skip_gain):
    length, chan_width = x_pair.shape
    head_count = decay_rate.shape[0]
    head_dim = chan_width // head_count
    state_dim = bc_pair.shape[1] // 2
    x_conv = conv_silu(x_pair.astype(jnp.float32), conv_x, conv_x_bias)
    bc_conv = conv_silu(bc_pair.astype(jnp.float32), conv_bc, conv_bc_bias)
    b_part = bc_conv[:, :state_dim]
    c_part = bc_conv[:, state_dim:]
    step_size = step_pair.astype(jnp.float32)
    log_decay = jnp.cumsum(-step_size * decay_rate[None, :], axis=0).T
    log_ratio = log_decay[:, :, None] - log_decay[:, None, :]
    later = jnp.arange(length, dtype=jnp.int32)[:, None]
    earlier = jnp.arange(length, dtype=jnp.int32)[None, :]
    causal = later >= earlier
    decay_mask = jnp.where(causal[None], jnp.exp(jnp.minimum(log_ratio, 0.0)), 0.0)
    scores = jnp.dot(c_part, b_part.T, precision=lax.Precision.HIGHEST, preferred_element_type=jnp.float32)
    weights = scores[None] * decay_mask * step_size.T[:, None, :]
    x_heads = x_conv.reshape(length, head_count, head_dim)
    mixed_out = jnp.einsum('hts,shp->thp', weights, x_heads, precision=lax.Precision.HIGHEST)
    mixed_out = mixed_out + skip_gain[None, :, None] * x_heads
    return mixed_out.reshape(length, chan_width).astype(jnp.bfloat16)

def reference(x_in, bc_in, dt_in, dt_bias, a_log, skip_d, conv_x, conv_x_bias, conv_bc, conv_bc_bias, norm_gain, lengths, dest_group, dest_slot):
    pair_total = N_GRP * PAIRS_GRP
    decay_rate = jnp.exp(a_log)
    targets = jnp.where(dest_group >= 0, dest_group * PAIRS_GRP + dest_slot, pair_total).astype(jnp.int32)
    sources = jnp.full((pair_total,), pair_total, jnp.int32).at[targets].set(jnp.arange(pair_total, dtype=jnp.int32), mode='drop')
    positions = jnp.arange(PAIR_LEN, dtype=jnp.int32)

    def one_slot(source):
        filled = source < pair_total
        pair_position_index = jnp.minimum(source, pair_total - 1).astype(jnp.int32)
        start = (pair_position_index * PAIR_LEN).astype(jnp.int32)
        x_rows = lax.dynamic_slice_in_dim(x_in, start, PAIR_LEN, 0)
        input_state_rows = lax.dynamic_slice_in_dim(bc_in, start, PAIR_LEN, 0)
        dt_rows = lax.dynamic_slice_in_dim(dt_in, start, PAIR_LEN, 0)
        valid = positions < lengths[pair_position_index]
        x_masked = jnp.where(valid[:, None], x_rows, jnp.zeros_like(x_rows))
        bc_masked = jnp.where(valid[:, None], input_state_rows, jnp.zeros_like(input_state_rows))
        step_rows = (jax.nn.softplus(dt_rows.astype(jnp.float32) + dt_bias[None, :]) * valid[:, None].astype(jnp.float32)).astype(jnp.bfloat16)
        mixed = mix_pair(x_masked, bc_masked, step_rows, conv_x, conv_x_bias, conv_bc, conv_bc_bias, decay_rate, skip_d)
        values = mixed.astype(jnp.float32)
        scale = lax.rsqrt(lax.optimization_barrier(jnp.mean(values * values, axis=1, keepdims=True)) + 1e-05)
        normed = values * scale * norm_gain[None, :]
        return jnp.where(filled, normed, jnp.zeros_like(normed)).astype(jnp.bfloat16)
    placed = lax.map(one_slot, sources)
    return placed.reshape(pair_total * PAIR_LEN, INNER)
```

```python
import functools

import jax
import jax.numpy as jnp
from jax import lax
from jax.experimental import pallas as pl
from jax.experimental.pallas import tpu as pltpu
from jax.sharding import PartitionSpec as P

LEVELS = (128, 144, 160, 176, 192, 208, 224, 240, 256)
LOG2E = 1.4426950408889634
F32 = jnp.float32
BF16 = jnp.bfloat16


def conv_silu(values, taps, bias, rows):
    count = 4
    total = jnp.broadcast_to(bias, values.shape)
    for k in range(count):
        back = count - 1 - k
        moved = values
        if back:
            moved = jnp.where(rows >= back, pltpu.roll(values, back, 0), 0.0)
        total = total + taps[k : k + 1] * moved
    return total / (1.0 + jnp.exp(-total))


def mix_kernel(
    heads, spread, sc, x_own, x_oth, bc_own, bc_oth, w, wbc, step, neg, out, scores, decay
):
    core, used = sc[0], sc[1]
    j = pl.program_id(0)
    half = x_own.shape[0]
    length = 2 * half
    width = x_own.shape[1]

    def joined(own, oth):
        own, oth = own.astype(F32), oth.astype(F32)
        low = jnp.where(core == 0, own, oth)
        high = jnp.where(core == 0, oth, own)
        both = jnp.concatenate([low, high], axis=0)
        rows = lax.broadcasted_iota(jnp.int32, both.shape, 0)
        return jnp.where(rows < used, both, 0.0), rows

    @pl.when(j == 0)
    def _():
        bc, rows = joined(bc_own[...], bc_oth[...])
        act = conv_silu(bc, wbc[0:4], wbc[4:5], rows)
        state = act.shape[1] // 2
        later = lax.broadcasted_iota(jnp.int32, (length, length), 0)
        earlier = lax.broadcasted_iota(jnp.int32, (length, length), 1)
        raw = lax.dot_general(
            act[:, state:],
            act[:, :state],
            (((1,), (1,)), ((), ())),
            precision=lax.Precision.HIGHEST,
            preferred_element_type=F32,
        )
        scores[...] = jnp.where(later >= earlier, raw, 0.0)
        upper = jnp.where(later <= earlier, 1.0, 0.0).astype(F32)
        decay[...] = LOG2E * jnp.dot(
            neg[...], upper, precision=lax.Precision.HIGHEST, preferred_element_type=F32
        )

    x, rows = joined(x_own[...], x_oth[...])
    x_act = conv_silu(x, w[0, 0:4], w[0, 4:5], rows)
    at = pl.ds(pl.multiple_of(8 * j, 8), 8)
    decay_rows = decay[at]
    decay_cols = jnp.transpose(decay_rows)
    step_cols = jnp.transpose(step[at])
    dim = width // heads
    mixed = []
    for h in range(heads):
        one = slice(h * dim, (h + 1) * dim)
        fed = x_act[:, one] * step_cols[:, h : h + 1]
        fed_hi = fed.astype(BF16)
        fed_lo = (fed - fed_hi.astype(F32)).astype(BF16)
        fed_both = jnp.concatenate([fed_hi, fed_lo], axis=1)
        parts = []
        for lo, hi in ((0, half), (half, length)):
            gap = decay_cols[lo:hi, h : h + 1] - decay_rows[h : h + 1, :hi]
            weight = scores[lo:hi, :hi] * jnp.exp2(jnp.minimum(gap, 0.0))
            both = jnp.dot(weight.astype(BF16), fed_both[:hi], preferred_element_type=F32)
            parts.append(both[:, :dim] + both[:, dim:])
        mixed.append(jnp.concatenate(parts, axis=0))
    result = jnp.concatenate(mixed, axis=1) + w[0, 5:6] * x_act
    keep = length // spread
    to = lax.broadcasted_iota(jnp.int32, (length, length), 0)
    source = lax.broadcasted_iota(jnp.int32, (length, length), 1)
    pick = jnp.where(source == (to % keep) * spread + to // keep, 1.0, 0.0).astype(BF16)
    out[0] = jnp.dot(pick, result.astype(BF16), preferred_element_type=F32).astype(BF16)


def one_hot(size, place):
    at = lax.broadcasted_iota(jnp.int32, (size, place.shape[1]), 0)
    return jnp.where(at == place, 1.0, 0.0).astype(BF16)


def packed(size, place, rows):
    return jnp.dot(one_hot(size, place), rows, preferred_element_type=F32).astype(BF16)


def unpacked(place, rows):
    pick = one_hot(rows.shape[0], place)
    return lax.dot_general(
        pick, rows, (((0,), (0,)), ((), ())), preferred_element_type=F32
    ).astype(BF16)


def pack_kernel(sc, rows, place, out):
    whole_rows = rows[...].reshape(place.shape[2], rows.shape[2])
    out[0] = packed(out.shape[1], place[0], whole_rows)


def repack_kernel(count, keep, source, rows, place_in, place_out, out, wide):
    z = pl.program_id(0)
    width = rows.shape[2]

    @pl.when(z == 0)
    def _():
        def widen(i, carry):
            wide[i] = unpacked(place_in[i], rows[i]).reshape(wide.shape[1:])
            return carry

        lax.fori_loop(0, rows.shape[0], widen, 0)

    blocks = []
    for g in range(count):
        i = source[z * count + g]
        blocks.append(wide[i // count, i % count])
    out[0] = packed(out.shape[1], place_out[0], jnp.concatenate(blocks, axis=0))


def unpack_kernel(sc, rows, place, out):
    out[...] = unpacked(place[0], rows[0]).reshape(out.shape)


def finish_kernel(spread, sc, rows, own, oth):
    core, last, filled = sc[0], sc[1], sc[2]
    length = rows.shape[1]
    half = length // 2
    keep = length // spread
    source = lax.broadcasted_iota(jnp.int32, (half, length), 1)
    index = lax.broadcasted_iota(jnp.int32, (half, length), 0)
    for first, out in ((core * half, own), ((1 - core) * half, oth)):
        t = jnp.minimum(index + first, last)
        place = (t % spread) * keep + t // spread
        pick = jnp.where((source == place) & (filled > 0), 1.0, 0.0).astype(BF16)
        out[...] = jnp.dot(pick, rows[0], preferred_element_type=F32).astype(BF16)


def norm_kernel(sc, own, oth, gain, out):
    core = sc[0]
    width = own.shape[1]
    mine, other = own[...].astype(F32), oth[...].astype(F32)
    total = jnp.sum(mine * mine, axis=1, keepdims=True) + jnp.sum(
        other * other, axis=1, keepdims=True
    )
    scale = lax.rsqrt(total / (2 * width) + 1e-05)
    for values, side in ((mine, core), (other, 1 - core)):
        at = pl.ds(pl.multiple_of(side * width, width), width)
        out[:, at] = (values * scale * gain[:, at]).astype(BF16)


def grid_spec(scalars, grid, ins, outs, scratch=()):
    return pltpu.PrefetchScalarGridSpec(
        num_scalar_prefetch=scalars,
        grid=grid,
        in_specs=ins,
        out_specs=outs,
        scratch_shapes=list(scratch),
    )


def whole(shape):
    return pl.BlockSpec(shape, lambda *_: (0,) * len(shape))


def per_device(
    x_in,
    bc_in,
    dt_in,
    dt_bias,
    a_log,
    skip_d,
    conv_x,
    conv_x_bias,
    conv_bc,
    conv_bc_bias,
    norm_gain,
    lengths,
    dest_group,
    dest_slot,
):
    n_ch = lax.axis_size("ch")
    n_grp = lax.axis_size("grp")
    n_z = n_ch // 2
    me = lax.axis_index("ch")
    my_group = lax.axis_index("grp")
    my_z, core = me // 2, me % 2
    half, channels = x_in.shape
    length = 2 * half
    mine = channels // 2
    width = channels // n_ch
    heads = a_log.shape[0]
    head_dim = width // heads
    head_half = dt_in.shape[1] // 2
    chunks = mine // width
    keep = length // n_z
    swap = [(i, i ^ 1) for i in range(n_ch)]
    rings = [[2 * z + c for z in range(n_z)] for c in range(2)]

    other_half = 1 - core
    x_oth = lax.ppermute(
        lax.dynamic_slice_in_dim(x_in, other_half * mine, mine, 1), "ch", swap
    )
    bc_oth = lax.ppermute(bc_in, "ch", swap)
    dt_oth = lax.ppermute(
        lax.dynamic_slice_in_dim(dt_in, other_half * head_half, head_half, 1), "ch", swap
    )
    small = jnp.concatenate(
        [
            conv_x,
            conv_x_bias[None],
            jnp.repeat(skip_d, head_dim)[None],
            jnp.repeat(a_log, head_dim)[None],
            jnp.zeros((1, width), F32),
        ],
        axis=0,
    )
    w_all = lax.all_to_all(
        jnp.broadcast_to(small[None], (n_ch, 8, width)), "ch", split_axis=0, concat_axis=0, tiled=True
    )

    pairs = n_grp * n_z
    ids = jnp.arange(pairs, dtype=jnp.int32)
    alive = dest_group >= 0
    units = jnp.where(alive, (jnp.minimum(lengths + 4, length) + n_z - 1) // n_z, 0)
    by_group = units.reshape(n_grp, n_z)
    ends = jnp.cumsum(by_group, axis=0)
    starts = ends - by_group
    target = jnp.where(alive, dest_group * n_z + dest_slot, pairs)
    match = target[None, :] == ids[:, None]

    def looked_up(values):
        return jnp.sum(jnp.where(match, values[None, :], 0), axis=1)

    to_units = looked_up(units).reshape(n_grp, n_z)
    slot_len = looked_up(lengths)
    source = looked_up((ids % n_z) * n_grp + ids // n_z)
    to_ends = jnp.cumsum(to_units, axis=0)
    to_starts = to_ends - to_units
    needed = jnp.maximum(jnp.max(ends[-1]), jnp.max(to_ends[-1]))

    def places(count, start):
        k = jnp.arange(keep, dtype=jnp.int32)
        at = jnp.where(k < count.T[:, :, None], start.T[:, :, None] + k, -1)
        return at.reshape(n_z, 1, n_grp * keep)

    place_from = places(by_group, starts)
    place_to = places(to_units, to_starts)
    source = source.reshape(n_grp, n_z).T.reshape(-1)
    z_only = my_z[None].astype(jnp.int32)

    my_dt = lax.dynamic_slice_in_dim(dt_in, core * head_half, head_half, 1)
    dt_both = jnp.concatenate(
        [jnp.where(core == 0, my_dt, dt_oth), jnp.where(core == 0, dt_oth, my_dt)], axis=0
    )
    used = lengths[my_group * n_z + my_z]
    valid = jnp.arange(length, dtype=jnp.int32) < used
    bias = lax.dynamic_slice_in_dim(dt_bias, core * head_half, head_half, 0)
    step = (
        jax.nn.softplus(dt_both.astype(F32) + bias[None, :]) * valid[:, None].astype(F32)
    ).astype(BF16).astype(F32)
    rate_all = jnp.exp(w_all[:, 6, ::head_dim])
    rate = lax.dynamic_slice_in_dim(rate_all, core * chunks, chunks, 0)

    def by_chunk(a):
        a = a.reshape(chunks, heads, length)
        return jnp.pad(a, ((0, 0), (0, 8 - heads), (0, 0))).reshape(chunks * 8, length)

    step_t = by_chunk(step.T)
    neg_t = by_chunk(-step.T * rate.reshape(-1)[:, None])
    wbc = jnp.concatenate([conv_bc, conv_bc_bias[None], jnp.zeros((3, conv_bc.shape[1]), F32)], axis=0)

    mixed = pl.pallas_call(
        functools.partial(mix_kernel, heads, n_z),
        out_shape=jax.ShapeDtypeStruct((chunks, length, width), BF16),
        grid_spec=grid_spec(
            1,
            (chunks,),
            [
                pl.BlockSpec((half, width), lambda j, sc: (0, sc[0] * chunks + j)),
                pl.BlockSpec((half, width), lambda j, sc: (0, j)),
                whole(bc_in.shape),
                whole(bc_in.shape),
                pl.BlockSpec((1, 8, width), lambda j, sc: (sc[0] * chunks + j, 0, 0)),
                whole(wbc.shape),
                whole(step_t.shape),
                whole(neg_t.shape),
            ],
            pl.BlockSpec((1, length, width), lambda j, sc: (j, 0, 0)),
            [pltpu.VMEM((length, length), F32), pltpu.VMEM((chunks * 8, length), F32)],
        ),
        name="mix",
    )(jnp.stack([core, used]).astype(jnp.int32), x_in, x_oth, bc_in, bc_oth, w_all, wbc, step_t, neg_t)

    spread = lax.all_to_all(mixed, "grp", split_axis=0, concat_axis=0, tiled=True)

    def route(size, spread):
        def exchange(a):
            return lax.all_to_all(
                a, "ch", split_axis=0, concat_axis=0, axis_index_groups=rings, tiled=True
            )

        one_place = pl.BlockSpec((1, 1, n_grp * keep), lambda i, sc: (sc[0], 0, 0))
        by_z = pl.BlockSpec((1, size, width), lambda i, *_: (i, 0, 0))
        strided = pl.BlockSpec((n_grp, keep, width), lambda i, *_: (0, i, 0))
        short = jax.ShapeDtypeStruct((n_z, size, width), BF16)
        outgoing = pl.pallas_call(
            pack_kernel,
            out_shape=short,
            grid_spec=grid_spec(1, (n_z,), [strided, one_place], by_z),
            name="pack",
        )(z_only, spread, place_from)
        ordered = pl.pallas_call(
            functools.partial(repack_kernel, n_grp, keep),
            out_shape=short,
            grid_spec=grid_spec(
                1,
                (n_z,),
                [
                    whole((n_z, size, width)),
                    whole(place_from.shape),
                    pl.BlockSpec((1, 1, n_grp * keep), lambda i, sc: (i, 0, 0)),
                ],
                by_z,
                [pltpu.VMEM((n_z, n_grp, keep, width), BF16)],
            ),
            name="repack",
        )(source, exchange(outgoing), place_from, place_to)
        return pl.pallas_call(
            unpack_kernel,
            out_shape=jax.ShapeDtypeStruct((n_grp, length, width), BF16),
            grid_spec=grid_spec(1, (n_z,), [by_z, one_place], strided),
            name="unpack",
        )(z_only, exchange(ordered), place_to)

    sizes = [s for s in LEVELS if s < n_grp * keep] + [n_grp * keep]
    level = jnp.sum((needed > jnp.array(sizes[:-1], jnp.int32)).astype(jnp.int32))
    landed = lax.switch(level, [functools.partial(route, s) for s in sizes], spread)
    rows = lax.all_to_all(landed, "grp", split_axis=0, concat_axis=0, tiled=True)

    slot = my_group * n_z + my_z
    last = jnp.minimum(slot_len[slot] + 3, length - 1)
    filled = jnp.any(target == slot)
    ends_at = jnp.stack([core, last, filled.astype(jnp.int32)]).astype(jnp.int32)
    own, oth = pl.pallas_call(
        functools.partial(finish_kernel, n_z),
        out_shape=[jax.ShapeDtypeStruct((half, mine), BF16)] * 2,
        grid_spec=grid_spec(
            1,
            (chunks,),
            [pl.BlockSpec((1, length, width), lambda j, sc: (j, 0, 0))],
            [pl.BlockSpec((half, width), lambda j, sc: (0, j))] * 2,
        ),
        name="finish",
    )(ends_at, rows)
    got = lax.ppermute(oth, "ch", swap)
    step_rows = 16
    return pl.pallas_call(
        norm_kernel,
        out_shape=jax.ShapeDtypeStruct((half, channels), BF16),
        grid_spec=grid_spec(
            1,
            (half // step_rows,),
            [pl.BlockSpec((step_rows, mine), lambda i, sc: (i, 0))] * 2 + [whole((1, channels))],
            pl.BlockSpec((step_rows, channels), lambda i, sc: (i, 0)),
        ),
        name="norm",
    )(ends_at, own, got, norm_gain[None])


def solution(mesh):
    placed = (
        P(("grp", "ch"), None),
        P(("grp", "ch"), None),
        P(("grp", "ch"), None),
        P(),
        P("ch"),
        P("ch"),
        P(None, "ch"),
        P("ch"),
        P(),
        P(),
        P(),
        P(),
        P(),
        P(),
    )
    return jax.shard_map(
        per_device, mesh=mesh, in_specs=placed, out_specs=P(("grp", "ch"), None), check_vma=False
    )
```

```python
import functools

import jax
import jax.numpy as jnp
from jax import lax
from jax.experimental import pallas as pl
from jax.experimental.pallas import tpu as pltpu
from jax.sharding import PartitionSpec as P

LEVELS = (96, 128, 144, 152, 160, 168, 176, 184, 192, 200, 208, 224)
LOG2E = 1.4426950408889634
F32 = jnp.float32
BF16 = jnp.bfloat16


def conv_silu(values, taps, bias, rows):
    count = 4
    total = jnp.broadcast_to(bias, values.shape)
    for k in range(count):
        back = count - 1 - k
        moved = values
        if back:
            moved = jnp.where(rows >= back, pltpu.roll(values, back, 0), 0.0)
        total = total + taps[k : k + 1] * moved
    low = 0.5 * total
    return low + low * jnp.tanh(low)


def mix_kernel(
    heads, spread, sc, x_own, x_oth, bc_own, bc_oth, w, wbc, step, neg, out,
    scores, decay, pick, joint, joint_bc,
):
    core, used = sc[0], sc[1]
    j = pl.program_id(0)
    half, width = x_own.shape
    length = 2 * half

    def joined(own, oth, buffer):
        buffer[core] = own[...]
        buffer[1 - core] = oth[...]
        both = buffer[...].reshape(length, own.shape[1]).astype(F32)
        rows = lax.broadcasted_iota(jnp.int32, both.shape, 0)
        return jnp.where(rows < used, both, 0.0), rows

    @pl.when(j == 0)
    def _():
        bc, rows = joined(bc_own, bc_oth, joint_bc)
        act = conv_silu(bc, wbc[0:4], wbc[4:5], rows)
        state = act.shape[1] // 2
        later = lax.broadcasted_iota(jnp.int32, (length, length), 0)
        earlier = lax.broadcasted_iota(jnp.int32, (length, length), 1)
        raw = lax.dot_general(
            act[:, state:],
            act[:, :state],
            (((1,), (1,)), ((), ())),
            precision=lax.Precision.HIGHEST,
            preferred_element_type=F32,
        )
        scores[...] = jnp.where(later >= earlier, raw, 0.0)
        upper = jnp.where(later <= earlier, 1.0, 0.0).astype(F32)
        decay[...] = LOG2E * jnp.dot(
            neg[...], upper, precision=lax.Precision.HIGHEST, preferred_element_type=F32
        )
        keep = length // spread
        place = (later % keep) * spread + later // keep
        pick[...] = jnp.where(earlier == place, 1.0, 0.0).astype(BF16)

    x, rows = joined(x_own, x_oth, joint)
    x_act = conv_silu(x, w[0, 0:4], w[0, 4:5], rows)
    at = pl.ds(pl.multiple_of(8 * j, 8), 8)
    decay_rows = decay[at]
    decay_cols = jnp.transpose(decay_rows)
    step_cols = jnp.transpose(step[at])
    dim = width // heads
    pair = 2 * dim
    first = lax.broadcasted_iota(jnp.int32, (length, pair), 1) < dim
    mixed = []
    for p in range(heads // 2):
        steps = jnp.where(
            first, step_cols[:, 2 * p : 2 * p + 1], step_cols[:, 2 * p + 1 : 2 * p + 2]
        )
        fed = x_act[:, p * pair : (p + 1) * pair] * steps
        fed_hi = fed.astype(BF16)
        fed_lo = (fed - fed_hi.astype(F32)).astype(BF16)
        fed_both = jnp.concatenate([fed_hi, fed_lo], axis=1)
        sums = []
        for h in (2 * p, 2 * p + 1):
            parts = []
            for lo, hi in ((0, half), (half, length)):
                gap = decay_cols[lo:hi, h : h + 1] - decay_rows[h : h + 1, :hi]
                weight = scores[lo:hi, :hi] * jnp.exp2(jnp.minimum(gap, 0.0))
                both = jnp.dot(weight.astype(BF16), fed_both[:hi], preferred_element_type=F32)
                parts.append(both[:, :pair] + both[:, pair:])
            sums.append(jnp.concatenate(parts, axis=0))
        mixed.append(jnp.where(first, sums[0], sums[1]))
    result = jnp.concatenate(mixed, axis=1) + w[0, 5:6] * x_act
    out[0] = jnp.dot(pick[...], result.astype(BF16), preferred_element_type=F32).astype(BF16)


def one_hot(size, place):
    at = lax.broadcasted_iota(jnp.int32, (size, place.shape[1]), 0)
    return jnp.where(at == place, 1.0, 0.0).astype(BF16)


def one_hot_back(size, place):
    count = place.shape[1]
    column = jnp.transpose(jnp.broadcast_to(place.astype(F32), (8, count)))[:, :1]
    at = lax.broadcasted_iota(jnp.int32, (count, size), 1).astype(F32)
    return jnp.where(at == column, 1.0, 0.0).astype(BF16)


def chosen(pick, rows):
    return jnp.dot(pick, rows, preferred_element_type=F32).astype(BF16)


def pack_kernel(sc, rows, place, out, pick):
    @pl.when(pl.program_id(0) == 0)
    def _():
        pick[...] = one_hot(out.shape[1], place[0])

    out[0] = chosen(pick[...], rows[...].reshape(place.shape[2], rows.shape[2]))


def widen_kernel(rows, place, out):
    one = chosen(one_hot_back(rows.shape[1], place[0]), rows[0])
    out[0] = one.reshape(out.shape[1:])


def order_kernel(count, source, rows, place, out):
    z = pl.program_id(0)
    blocks = []
    for g in range(count):
        i = source[z * count + g]
        blocks.append(rows[i // count, i % count])
    out[0] = chosen(one_hot(out.shape[1], place[0]), jnp.concatenate(blocks, axis=0))


def unpack_kernel(sc, rows, place, out, pick):
    @pl.when(pl.program_id(0) == 0)
    def _():
        pick[...] = one_hot_back(rows.shape[1], place[0])

    out[...] = chosen(pick[...], rows[0]).reshape(out.shape)


def finish_kernel(spread, sc, rows, own, oth, pick):
    core, last, filled = sc[0], sc[1], sc[2]
    length = rows.shape[1]
    half = length // 2
    keep = length // spread

    @pl.when(pl.program_id(0) == 0)
    def _():
        source = lax.broadcasted_iota(jnp.int32, (length, length), 1)
        index = lax.broadcasted_iota(jnp.int32, (length, length), 0)
        swapped = jnp.where(index < half, index + half, index - half)
        t = jnp.minimum(jnp.where(core == 0, index, swapped), last)
        place = (t % spread) * keep + t // spread
        pick[...] = jnp.where((source == place) & (filled > 0), 1.0, 0.0).astype(BF16)

    picked = chosen(pick[...], rows[0])
    own[...] = picked[:half]
    oth[...] = picked[half:]


def norm_kernel(sc, own, oth, gain, out):
    core = sc[0]
    width = own.shape[1]
    mine, other = own[...].astype(F32), oth[...].astype(F32)
    total = jnp.sum(mine * mine, axis=1, keepdims=True) + jnp.sum(
        other * other, axis=1, keepdims=True
    )
    scale = lax.rsqrt(total / (2 * width) + 1e-05)
    for values, side in ((mine, core), (other, 1 - core)):
        at = pl.ds(pl.multiple_of(side * width, width), width)
        out[:, at] = (values * scale * gain[:, at]).astype(BF16)


def grid_spec(scalars, grid, ins, outs, scratch=()):
    return pltpu.PrefetchScalarGridSpec(
        num_scalar_prefetch=scalars,
        grid=grid,
        in_specs=ins,
        out_specs=outs,
        scratch_shapes=list(scratch),
    )


def whole(shape):
    return pl.BlockSpec(shape, lambda *_: (0,) * len(shape))


def per_device(
    x_in,
    bc_in,
    dt_in,
    dt_bias,
    a_log,
    skip_d,
    conv_x,
    conv_x_bias,
    conv_bc,
    conv_bc_bias,
    norm_gain,
    lengths,
    dest_group,
    dest_slot,
):
    n_ch = lax.axis_size("ch")
    n_grp = lax.axis_size("grp")
    n_z = n_ch // 2
    me = lax.axis_index("ch")
    my_group = lax.axis_index("grp")
    my_z, core = me // 2, me % 2
    half, channels = x_in.shape
    length = 2 * half
    mine = channels // 2
    width = channels // n_ch
    heads = a_log.shape[0]
    head_dim = width // heads
    head_half = dt_in.shape[1] // 2
    chunks = mine // width
    keep = length // n_z
    swap = [(i, i ^ 1) for i in range(n_ch)]
    rings = [[2 * z + c for z in range(n_z)] for c in range(2)]

    other_half = 1 - core
    x_oth = lax.ppermute(
        lax.dynamic_slice_in_dim(x_in, other_half * mine, mine, 1), "ch", swap
    )
    bc_oth = lax.ppermute(bc_in, "ch", swap)
    dt_oth = lax.ppermute(
        lax.dynamic_slice_in_dim(dt_in, other_half * head_half, head_half, 1), "ch", swap
    )
    small = jnp.concatenate(
        [
            conv_x,
            conv_x_bias[None],
            jnp.repeat(skip_d, head_dim)[None],
            jnp.repeat(a_log, head_dim)[None],
            jnp.zeros((1, width), F32),
        ],
        axis=0,
    )
    small_oth = lax.ppermute(small, "ch", swap)
    shares = jnp.stack(
        [jnp.where(core == 0, small, small_oth), jnp.where(core == 0, small_oth, small)]
    )

    def exchange(a):
        return lax.all_to_all(
            a, "ch", split_axis=0, concat_axis=0, axis_index_groups=rings, tiled=True
        )

    w_all = exchange(jnp.broadcast_to(shares[None], (n_z, 2, 8, width))).reshape(n_ch, 8, width)

    pairs = n_grp * n_z
    ids = jnp.arange(pairs, dtype=jnp.int32)
    alive = dest_group >= 0
    units = jnp.where(alive, (jnp.minimum(lengths + 4, length) + n_z - 1) // n_z, 0)
    by_group = units.reshape(n_grp, n_z)
    ends = jnp.cumsum(by_group, axis=0)
    starts = ends - by_group
    target = jnp.where(alive, dest_group * n_z + dest_slot, pairs)
    match = target[None, :] == ids[:, None]

    def looked_up(values):
        return jnp.sum(jnp.where(match, values[None, :], 0), axis=1)

    to_units = looked_up(units).reshape(n_grp, n_z)
    slot_len = looked_up(lengths)
    source = looked_up((ids % n_z) * n_grp + ids // n_z)
    to_ends = jnp.cumsum(to_units, axis=0)
    to_starts = to_ends - to_units

    def places(count, start):
        k = jnp.arange(keep, dtype=jnp.int32)
        at = jnp.where(k < count.T[:, :, None], start.T[:, :, None] + k, -1)
        return at.reshape(n_z, 1, n_grp * keep)

    place_from = places(by_group, starts)
    place_to = places(to_units, to_starts)
    source = source.reshape(n_grp, n_z).T.reshape(-1)
    z_only = my_z[None].astype(jnp.int32)

    my_dt = lax.dynamic_slice_in_dim(dt_in, core * head_half, head_half, 1)
    dt_both = jnp.concatenate(
        [jnp.where(core == 0, my_dt, dt_oth), jnp.where(core == 0, dt_oth, my_dt)], axis=0
    )
    used = lengths[my_group * n_z + my_z]
    valid = jnp.arange(length, dtype=jnp.int32) < used
    bias = lax.dynamic_slice_in_dim(dt_bias, core * head_half, head_half, 0)
    step = (
        jax.nn.softplus(dt_both.astype(F32) + bias[None, :]) * valid[:, None].astype(F32)
    ).astype(BF16).astype(F32)
    rate_all = jnp.exp(w_all[:, 6, ::head_dim])
    rate = lax.dynamic_slice_in_dim(rate_all, core * chunks, chunks, 0)

    def by_chunk(a):
        a = a.reshape(chunks, heads, length)
        return jnp.pad(a, ((0, 0), (0, 8 - heads), (0, 0))).reshape(chunks * 8, length)

    step_t = by_chunk(step.T)
    neg_t = by_chunk(-step.T * rate.reshape(-1)[:, None])
    wbc = jnp.concatenate([conv_bc, conv_bc_bias[None], jnp.zeros((3, conv_bc.shape[1]), F32)], axis=0)

    mixed = pl.pallas_call(
        functools.partial(mix_kernel, heads, n_z),
        out_shape=jax.ShapeDtypeStruct((chunks, length, width), BF16),
        grid_spec=grid_spec(
            1,
            (chunks,),
            [
                pl.BlockSpec((half, width), lambda j, sc: (0, sc[0] * chunks + j)),
                pl.BlockSpec((half, width), lambda j, sc: (0, j)),
                whole(bc_in.shape),
                whole(bc_in.shape),
                pl.BlockSpec((1, 8, width), lambda j, sc: (sc[0] * chunks + j, 0, 0)),
                whole(wbc.shape),
                whole(step_t.shape),
                whole(neg_t.shape),
            ],
            pl.BlockSpec((1, length, width), lambda j, sc: (j, 0, 0)),
            [
                pltpu.VMEM((length, length), F32),
                pltpu.VMEM((chunks * 8, length), F32),
                pltpu.VMEM((length, length), BF16),
                pltpu.VMEM((2, half, width), BF16),
                pltpu.VMEM((2,) + bc_in.shape, BF16),
            ],
        ),
        name="mix",
    )(jnp.stack([core, used]).astype(jnp.int32), x_in, x_oth, bc_in, bc_oth, w_all, wbc, step_t, neg_t)

    spread = lax.all_to_all(mixed, "grp", split_axis=0, concat_axis=0, tiled=True)

    full = n_grp * keep
    my_place = pl.BlockSpec((1, 1, full), lambda i, sc: (sc[0], 0, 0))
    each_place = pl.BlockSpec((1, 1, full), lambda i, *_: (i, 0, 0))
    strided = pl.BlockSpec((n_grp, keep, width), lambda i, *_: (0, i, 0))
    wide_shape = (n_z, n_grp, keep, width)

    def by_z(size):
        return pl.BlockSpec((1, size, width), lambda i, *_: (i, 0, 0))

    def short(size):
        return jax.ShapeDtypeStruct((n_z, size, width), BF16)

    def outward(size, spread):
        outgoing = pl.pallas_call(
            pack_kernel,
            out_shape=short(size),
            grid_spec=grid_spec(
                1, (n_z,), [strided, my_place], by_z(size), [pltpu.VMEM((size, full), BF16)]
            ),
            name="pack",
        )(z_only, spread, place_from)
        return pl.pallas_call(
            widen_kernel,
            out_shape=jax.ShapeDtypeStruct(wide_shape, BF16),
            grid_spec=grid_spec(
                0,
                (n_z,),
                [by_z(size), each_place],
                pl.BlockSpec((1,) + wide_shape[1:], lambda i: (i, 0, 0, 0)),
            ),
            name="widen",
        )(exchange(outgoing), place_from)

    def homeward(size, wide):
        ordered = pl.pallas_call(
            functools.partial(order_kernel, n_grp),
            out_shape=short(size),
            grid_spec=grid_spec(1, (n_z,), [whole(wide_shape), each_place], by_z(size)),
            name="order",
        )(source, wide, place_to)
        return pl.pallas_call(
            unpack_kernel,
            out_shape=jax.ShapeDtypeStruct((n_grp, length, width), BF16),
            grid_spec=grid_spec(
                1, (n_z,), [by_z(size), my_place], strided, [pltpu.VMEM((full, size), BF16)]
            ),
            name="unpack",
        )(z_only, exchange(ordered), place_to)

    sizes = [s for s in LEVELS if s < full] + [full]

    def sized(step, needed, rows):
        level = jnp.sum((jnp.max(needed) > jnp.array(sizes[:-1], jnp.int32)).astype(jnp.int32))
        return lax.switch(level, [functools.partial(step, s) for s in sizes], rows)

    wide = sized(outward, ends[-1], spread)
    landed = sized(homeward, to_ends[-1], wide)
    rows = lax.all_to_all(landed, "grp", split_axis=0, concat_axis=0, tiled=True)

    slot = my_group * n_z + my_z
    last = jnp.minimum(slot_len[slot] + 3, length - 1)
    filled = jnp.any(target == slot)
    ends_at = jnp.stack([core, last, filled.astype(jnp.int32)]).astype(jnp.int32)
    own, oth = pl.pallas_call(
        functools.partial(finish_kernel, n_z),
        out_shape=[jax.ShapeDtypeStruct((half, mine), BF16)] * 2,
        grid_spec=grid_spec(
            1,
            (chunks,),
            [pl.BlockSpec((1, length, width), lambda j, sc: (j, 0, 0))],
            [pl.BlockSpec((half, width), lambda j, sc: (0, j))] * 2,
            [pltpu.VMEM((length, length), BF16)],
        ),
        name="finish",
    )(ends_at, rows)
    got = lax.ppermute(oth, "ch", swap)
    step_rows = 32
    return pl.pallas_call(
        norm_kernel,
        out_shape=jax.ShapeDtypeStruct((half, channels), BF16),
        grid_spec=grid_spec(
            1,
            (half // step_rows,),
            [pl.BlockSpec((step_rows, mine), lambda i, sc: (i, 0))] * 2 + [whole((1, channels))],
            pl.BlockSpec((step_rows, channels), lambda i, sc: (i, 0)),
        ),
        name="norm",
    )(ends_at, own, got, norm_gain[None])


def solution(mesh):
    placed = (
        P(("grp", "ch"), None),
        P(("grp", "ch"), None),
        P(("grp", "ch"), None),
        P(),
        P("ch"),
        P("ch"),
        P(None, "ch"),
        P("ch"),
        P(),
        P(),
        P(),
        P(),
        P(),
        P(),
    )
    return jax.shard_map(
        per_device, mesh=mesh, in_specs=placed, out_specs=P(("grp", "ch"), None), check_vma=False
    )
```

```python
import functools

import jax
import jax.numpy as jnp
from jax import lax
from jax.experimental import pallas as pl
from jax.experimental.pallas import tpu as pltpu
from jax.sharding import PartitionSpec as P

LEVELS = (128, 152, 160, 168, 176, 184, 192, 200, 216)
LOG2E = 1.4426950408889634
F32 = jnp.float32
BF16 = jnp.bfloat16


def conv_silu(values, taps, bias, rows):
    count = 4
    total = jnp.broadcast_to(bias, values.shape)
    for k in range(count):
        back = count - 1 - k
        moved = values
        if back:
            moved = jnp.where(rows >= back, pltpu.roll(values, back, 0), 0.0)
        total = total + taps[k : k + 1] * moved
    low = 0.5 * total
    return low + low * jnp.tanh(low)


def mix_kernel(
    heads, spread, sc, x_own, x_oth, bc_own, bc_oth, w, wbc, step, neg, out,
    scores, decay, pick, joint, joint_bc,
):
    core, used = sc[0], sc[1]
    j = pl.program_id(0)
    half, width = x_own.shape
    length = 2 * half

    def joined(own, oth, buffer):
        buffer[core] = own[...]
        buffer[1 - core] = oth[...]
        both = buffer[...].reshape(length, own.shape[1]).astype(F32)
        rows = lax.broadcasted_iota(jnp.int32, both.shape, 0)
        return jnp.where(rows < used, both, 0.0), rows

    @pl.when(j == 0)
    def _():
        bc, rows = joined(bc_own, bc_oth, joint_bc)
        act = conv_silu(bc, wbc[0:4], wbc[4:5], rows)
        state = act.shape[1] // 2
        later = lax.broadcasted_iota(jnp.int32, (length, length), 0)
        earlier = lax.broadcasted_iota(jnp.int32, (length, length), 1)
        raw = lax.dot_general(
            act[:, state:],
            act[:, :state],
            (((1,), (1,)), ((), ())),
            precision=lax.Precision.HIGHEST,
            preferred_element_type=F32,
        )
        scores[...] = jnp.where(later >= earlier, raw, 0.0)
        upper = jnp.where(later <= earlier, 1.0, 0.0).astype(F32)
        decay[...] = LOG2E * jnp.dot(
            neg[...], upper, precision=lax.Precision.HIGHEST, preferred_element_type=F32
        )
        keep = length // spread
        place = (later % keep) * spread + later // keep
        pick[...] = jnp.where(earlier == place, 1.0, 0.0).astype(BF16)

    x, rows = joined(x_own, x_oth, joint)
    x_act = conv_silu(x, w[0, 0:4], w[0, 4:5], rows)
    at = pl.ds(pl.multiple_of(8 * j, 8), 8)
    decay_rows = decay[at]
    decay_cols = jnp.transpose(decay_rows)
    step_cols = jnp.transpose(step[at])
    dim = width // heads
    pair = 2 * dim
    first = lax.broadcasted_iota(jnp.int32, (length, pair), 1) < dim
    mixed = []
    for p in range(heads // 2):
        steps = jnp.where(
            first, step_cols[:, 2 * p : 2 * p + 1], step_cols[:, 2 * p + 1 : 2 * p + 2]
        )
        fed = x_act[:, p * pair : (p + 1) * pair] * steps
        fed_hi = fed.astype(BF16)
        fed_lo = (fed - fed_hi.astype(F32)).astype(BF16)
        fed_both = jnp.concatenate([fed_hi, fed_lo], axis=1)
        sums = []
        for h in (2 * p, 2 * p + 1):
            parts = []
            for lo, hi in ((0, half), (half, length)):
                gap = decay_cols[lo:hi, h : h + 1] - decay_rows[h : h + 1, :hi]
                weight = scores[lo:hi, :hi] * jnp.exp2(jnp.minimum(gap, 0.0))
                both = jnp.dot(weight.astype(BF16), fed_both[:hi], preferred_element_type=F32)
                parts.append(both[:, :pair] + both[:, pair:])
            sums.append(jnp.concatenate(parts, axis=0))
        mixed.append(jnp.where(first, sums[0], sums[1]))
    result = jnp.concatenate(mixed, axis=1) + w[0, 5:6] * x_act
    out[0] = jnp.dot(pick[...], result.astype(BF16), preferred_element_type=F32).astype(BF16)


def one_hot(size, place):
    at = lax.broadcasted_iota(jnp.int32, (size, place.shape[1]), 0)
    return jnp.where(at == place, 1.0, 0.0).astype(BF16)


def one_hot_back(size, place):
    count = place.shape[1]
    column = jnp.transpose(jnp.broadcast_to(place.astype(F32), (8, count)))[:, :1]
    at = lax.broadcasted_iota(jnp.int32, (count, size), 1).astype(F32)
    return jnp.where(at == column, 1.0, 0.0).astype(BF16)


def chosen(pick, rows):
    return jnp.dot(pick, rows, preferred_element_type=F32).astype(BF16)


def loop(count, body):
    def step(i, carry):
        body(i)
        return carry

    lax.fori_loop(0, count, step, 0, unroll=2)


def pack_kernel(sc, rows, place, out):
    pick = one_hot(out.shape[1], place[sc[0]])

    def body(i):
        out[i] = chosen(pick, rows[:, i].reshape(place.shape[2], rows.shape[3]))

    loop(out.shape[0], body)


def widen_kernel(rows, place, out):
    def body(i):
        one = chosen(one_hot_back(rows.shape[1], place[i]), rows[i])
        out[i] = one.reshape(out.shape[1:])

    loop(out.shape[0], body)


def order_kernel(count, source, rows, place, out):
    def body(z):
        blocks = []
        for g in range(count):
            i = source[z * count + g]
            blocks.append(rows[i // count, i % count])
        out[z] = chosen(one_hot(out.shape[1], place[z]), jnp.concatenate(blocks, axis=0))

    loop(out.shape[0], body)


def unpack_kernel(sc, rows, place, out):
    pick = one_hot_back(rows.shape[1], place[sc[0]])

    def body(i):
        one = chosen(pick, rows[i])
        out[:, i] = one.reshape((out.shape[0],) + out.shape[2:])

    loop(rows.shape[0], body)


def finish_kernel(spread, sc, rows, own, oth):
    core, last, filled = sc[0], sc[1], sc[2]
    length, width = rows.shape[1:]
    half = length // 2
    keep = length // spread
    source = lax.broadcasted_iota(jnp.int32, (length, length), 1)
    index = lax.broadcasted_iota(jnp.int32, (length, length), 0)
    swapped = jnp.where(index < half, index + half, index - half)
    t = jnp.minimum(jnp.where(core == 0, index, swapped), last)
    place = (t % spread) * keep + t // spread
    pick = jnp.where((source == place) & (filled > 0), 1.0, 0.0).astype(BF16)

    def body(j):
        picked = chosen(pick, rows[j])
        at = pl.ds(pl.multiple_of(j * width, width), width)
        own[:, at] = picked[:half]
        oth[:, at] = picked[half:]

    loop(rows.shape[0], body)


def norm_kernel(sc, own, oth, gain, out):
    core = sc[0]
    width = own.shape[1]
    mine, other = own[...].astype(F32), oth[...].astype(F32)
    total = jnp.sum(mine * mine, axis=1, keepdims=True) + jnp.sum(
        other * other, axis=1, keepdims=True
    )
    scale = lax.rsqrt(total / (2 * width) + 1e-05)
    for values, side in ((mine, core), (other, 1 - core)):
        at = pl.ds(pl.multiple_of(side * width, width), width)
        out[:, at] = (values * scale * gain[:, at]).astype(BF16)


def grid_spec(scalars, grid, ins, outs, scratch=()):
    return pltpu.PrefetchScalarGridSpec(
        num_scalar_prefetch=scalars,
        grid=grid,
        in_specs=ins,
        out_specs=outs,
        scratch_shapes=list(scratch),
    )


def whole(shape):
    return pl.BlockSpec(shape, lambda *_: (0,) * len(shape))


def per_device(
    x_in,
    bc_in,
    dt_in,
    dt_bias,
    a_log,
    skip_d,
    conv_x,
    conv_x_bias,
    conv_bc,
    conv_bc_bias,
    norm_gain,
    lengths,
    dest_group,
    dest_slot,
):
    n_ch = lax.axis_size("ch")
    n_grp = lax.axis_size("grp")
    n_z = n_ch // 2
    me = lax.axis_index("ch")
    my_group = lax.axis_index("grp")
    my_z, core = me // 2, me % 2
    half, channels = x_in.shape
    length = 2 * half
    mine = channels // 2
    width = channels // n_ch
    heads = a_log.shape[0]
    head_dim = width // heads
    head_half = dt_in.shape[1] // 2
    chunks = mine // width
    keep = length // n_z
    swap = [(i, i ^ 1) for i in range(n_ch)]
    rings = [[2 * z + c for z in range(n_z)] for c in range(2)]

    other_half = 1 - core
    x_oth = lax.ppermute(
        lax.dynamic_slice_in_dim(x_in, other_half * mine, mine, 1), "ch", swap
    )
    bc_oth = lax.ppermute(bc_in, "ch", swap)
    dt_oth = lax.ppermute(
        lax.dynamic_slice_in_dim(dt_in, other_half * head_half, head_half, 1), "ch", swap
    )
    small = jnp.concatenate(
        [
            conv_x,
            conv_x_bias[None],
            jnp.repeat(skip_d, head_dim)[None],
            jnp.repeat(a_log, head_dim)[None],
            jnp.zeros((1, width), F32),
        ],
        axis=0,
    )
    def exchange(a):
        return lax.all_to_all(
            a, "ch", split_axis=0, concat_axis=0, axis_index_groups=rings, tiled=True
        )

    by_chip = exchange(jnp.broadcast_to(small[None], (n_z, 8, width)))
    n_half = n_z // 2
    w_own = lax.dynamic_slice_in_dim(by_chip, core * n_half, n_half, 0)
    w_oth = lax.ppermute(
        lax.dynamic_slice_in_dim(by_chip, other_half * n_half, n_half, 0), "ch", swap
    )
    w_mine = jnp.stack(
        [jnp.where(core == 0, w_own, w_oth), jnp.where(core == 0, w_oth, w_own)], axis=1
    ).reshape(n_z, 8, width)

    pairs = n_grp * n_z
    ids = jnp.arange(pairs, dtype=jnp.int32)
    alive = dest_group >= 0
    units = jnp.where(alive, (jnp.minimum(lengths + 4, length) + n_z - 1) // n_z, 0)
    by_group = units.reshape(n_grp, n_z)
    ends = jnp.cumsum(by_group, axis=0)
    starts = ends - by_group
    target = jnp.where(alive, dest_group * n_z + dest_slot, pairs)
    match = target[None, :] == ids[:, None]

    def looked_up(values):
        return jnp.sum(jnp.where(match, values[None, :], 0), axis=1)

    to_units = looked_up(units).reshape(n_grp, n_z)
    slot_len = looked_up(lengths)
    source = looked_up((ids % n_z) * n_grp + ids // n_z)
    to_ends = jnp.cumsum(to_units, axis=0)
    to_starts = to_ends - to_units

    def places(count, start):
        k = jnp.arange(keep, dtype=jnp.int32)
        at = jnp.where(k < count.T[:, :, None], start.T[:, :, None] + k, -1)
        return at.reshape(n_z, 1, n_grp * keep)

    place_from = places(by_group, starts)
    place_to = places(to_units, to_starts)
    source = source.reshape(n_grp, n_z).T.reshape(-1)
    z_only = my_z[None].astype(jnp.int32)

    my_dt = lax.dynamic_slice_in_dim(dt_in, core * head_half, head_half, 1)
    dt_both = jnp.concatenate(
        [jnp.where(core == 0, my_dt, dt_oth), jnp.where(core == 0, dt_oth, my_dt)], axis=0
    )
    used = lengths[my_group * n_z + my_z]
    valid = jnp.arange(length, dtype=jnp.int32) < used
    bias = lax.dynamic_slice_in_dim(dt_bias, core * head_half, head_half, 0)
    step = (
        jax.nn.softplus(dt_both.astype(F32) + bias[None, :]) * valid[:, None].astype(F32)
    ).astype(BF16).astype(F32)
    rate = jnp.exp(w_mine[:, 6, ::head_dim])

    def by_chunk(a):
        a = a.reshape(chunks, heads, length)
        return jnp.pad(a, ((0, 0), (0, 8 - heads), (0, 0))).reshape(chunks * 8, length)

    step_t = by_chunk(step.T)
    neg_t = by_chunk(-step.T * rate.reshape(-1)[:, None])
    wbc = jnp.concatenate([conv_bc, conv_bc_bias[None], jnp.zeros((3, conv_bc.shape[1]), F32)], axis=0)

    mixed = pl.pallas_call(
        functools.partial(mix_kernel, heads, n_z),
        out_shape=jax.ShapeDtypeStruct((chunks, length, width), BF16),
        grid_spec=grid_spec(
            1,
            (chunks,),
            [
                pl.BlockSpec((half, width), lambda j, sc: (0, sc[0] * chunks + j)),
                pl.BlockSpec((half, width), lambda j, sc: (0, j)),
                whole(bc_in.shape),
                whole(bc_in.shape),
                pl.BlockSpec((1, 8, width), lambda j, sc: (j, 0, 0)),
                whole(wbc.shape),
                whole(step_t.shape),
                whole(neg_t.shape),
            ],
            pl.BlockSpec((1, length, width), lambda j, sc: (j, 0, 0)),
            [
                pltpu.VMEM((length, length), F32),
                pltpu.VMEM((chunks * 8, length), F32),
                pltpu.VMEM((length, length), BF16),
                pltpu.VMEM((2, half, width), BF16),
                pltpu.VMEM((2,) + bc_in.shape, BF16),
            ],
        ),
        name="mix",
    )(jnp.stack([core, used]).astype(jnp.int32), x_in, x_oth, bc_in, bc_oth, w_mine, wbc, step_t, neg_t)

    spread = lax.all_to_all(mixed, "grp", split_axis=0, concat_axis=0, tiled=True)

    full = n_grp * keep
    by_pair = (n_grp, n_z, keep, width)
    wide_shape = (n_z, n_grp, keep, width)

    def once(kernel, scalars, shapes, *operands):
        many = isinstance(shapes, list)
        outs = [jax.ShapeDtypeStruct(shape, BF16) for shape in (shapes if many else [shapes])]
        specs = [whole(out.shape) for out in outs]
        return pl.pallas_call(
            kernel,
            out_shape=outs if many else outs[0],
            grid_spec=grid_spec(
                scalars,
                (1,),
                [whole(a.shape) for a in operands[scalars:]],
                specs if many else specs[0],
            ),
        )(*operands)

    def outward(size, spread):
        outgoing = once(
            pack_kernel, 1, (n_z, size, width), z_only, spread.reshape(by_pair), place_from
        )
        return once(widen_kernel, 0, wide_shape, exchange(outgoing), place_from)

    def homeward(size, wide):
        ordered = once(
            functools.partial(order_kernel, n_grp), 1, (n_z, size, width), source, wide, place_to
        )
        landed = once(unpack_kernel, 1, by_pair, z_only, exchange(ordered), place_to)
        return landed.reshape(n_grp, length, width)

    sizes = [s for s in LEVELS if s < full] + [full]

    def sized(step, needed, rows):
        level = jnp.sum((jnp.max(needed) > jnp.array(sizes[:-1], jnp.int32)).astype(jnp.int32))
        return lax.switch(level, [functools.partial(step, s) for s in sizes], rows)

    wide = sized(outward, ends[-1], spread)
    landed = sized(homeward, to_ends[-1], wide)
    rows = lax.all_to_all(landed, "grp", split_axis=0, concat_axis=0, tiled=True)

    slot = my_group * n_z + my_z
    last = jnp.minimum(slot_len[slot] + 3, length - 1)
    filled = jnp.any(target == slot)
    ends_at = jnp.stack([core, last, filled.astype(jnp.int32)]).astype(jnp.int32)
    own, oth = once(
        functools.partial(finish_kernel, n_z), 1, [(half, mine)] * 2, ends_at, rows
    )
    got = lax.ppermute(oth, "ch", swap)
    step_rows = 32
    return pl.pallas_call(
        norm_kernel,
        out_shape=jax.ShapeDtypeStruct((half, channels), BF16),
        grid_spec=grid_spec(
            1,
            (half // step_rows,),
            [pl.BlockSpec((step_rows, mine), lambda i, sc: (i, 0))] * 2 + [whole((1, channels))],
            pl.BlockSpec((step_rows, channels), lambda i, sc: (i, 0)),
        ),
        name="norm",
    )(ends_at, own, got, norm_gain[None])


def solution(mesh):
    placed = (
        P(("grp", "ch"), None),
        P(("grp", "ch"), None),
        P(("grp", "ch"), None),
        P(),
        P("ch"),
        P("ch"),
        P(None, "ch"),
        P("ch"),
        P(),
        P(),
        P(),
        P(),
        P(),
        P(),
    )
    return jax.shard_map(
        per_device, mesh=mesh, in_specs=placed, out_specs=P(("grp", "ch"), None), check_vma=False
    )
```

```python
import functools

import jax
import jax.numpy as jnp
from jax import lax
from jax.experimental import pallas as pl
from jax.experimental.pallas import tpu as pltpu
from jax.sharding import PartitionSpec as P

LEVELS = (128, 152, 160, 168, 176, 184, 192, 200, 216)
LOG2E = 1.4426950408889634
F32 = jnp.float32
BF16 = jnp.bfloat16


def conv_silu(values, taps, bias, rows):
    count = 4
    total = jnp.broadcast_to(bias, values.shape)
    for k in range(count):
        back = count - 1 - k
        moved = values
        if back:
            moved = jnp.where(rows >= back, pltpu.roll(values, back, 0), 0.0)
        total = total + taps[k : k + 1] * moved
    low = 0.5 * total
    return low + low * jnp.tanh(low)


def small_kernel(skip, rate, taps, bias, out):
    count, width = out.shape[0], out.shape[2]
    heads = skip.shape[0]
    lane = lax.broadcasted_iota(jnp.int32, (1, width), 1)

    def by_channel(values):
        spread = jnp.full((1, width), values[0], F32)
        for h in range(1, heads):
            spread = jnp.where(lane >= h * (width // heads), values[h], spread)
        return spread

    rows = [taps[...], bias[...], by_channel(skip), by_channel(rate), jnp.zeros((1, width), F32)]
    share = jnp.concatenate(rows, axis=0)
    for i in range(count):
        out[i] = share


def joined(core, used, own, oth, buffer):
    buffer[core] = own
    buffer[1 - core] = oth
    both = buffer[...].reshape(2 * own.shape[0], own.shape[1]).astype(F32)
    rows = lax.broadcasted_iota(jnp.int32, both.shape, 0)
    return jnp.where(rows < used, both, 0.0), rows


def prep_kernel(spread, sc, bc_own, bc_oth, wbc, step, scores, summed, pick, buffer):
    bc, rows = joined(sc[0], sc[1], bc_own[...], bc_oth[...], buffer)
    length = bc.shape[0]
    act = conv_silu(bc, wbc[0:4], wbc[4:5], rows)
    state = act.shape[1] // 2
    later = lax.broadcasted_iota(jnp.int32, (length, length), 0)
    earlier = lax.broadcasted_iota(jnp.int32, (length, length), 1)
    raw = lax.dot_general(
        act[:, state:],
        act[:, :state],
        (((1,), (1,)), ((), ())),
        precision=lax.Precision.HIGHEST,
        preferred_element_type=F32,
    )
    scores[...] = jnp.where(later >= earlier, raw, 0.0)
    upper = jnp.where(later <= earlier, 1.0, 0.0).astype(F32)
    summed[...] = LOG2E * jnp.dot(
        step[...], upper, precision=lax.Precision.HIGHEST, preferred_element_type=F32
    )
    keep = length // spread
    place = (later % keep) * spread + later // keep
    pick[...] = jnp.where(earlier == place, 1.0, 0.0).astype(BF16)


def mix_kernel(
    heads, sc, x_own, x_oth, w_own, w_oth, step, scores, summed, pick, out, joint
):
    core, used = sc[0], sc[1]
    j = pl.program_id(0)
    half, width = x_own.shape
    length = 2 * half
    columns = pl.ds(pl.multiple_of(j * width, width), width)
    x, rows = joined(core, used, x_own[...], x_oth[:, columns], joint)
    w = jnp.where(j % 2 == core, w_own[j // 2], w_oth[j // 2])
    x_act = conv_silu(x, w[0:4], w[4:5], rows)
    at = pl.ds(pl.multiple_of(8 * j, 8), 8)
    dim = width // heads
    rates = -jnp.exp(w[6:7])
    sums_here = summed[at]
    scaled = [sums_here[h : h + 1] * rates[:, h * dim : h * dim + 1] for h in range(heads)]
    decay_rows = jnp.concatenate(scaled + [sums_here[heads:]], axis=0)
    decay_cols = jnp.transpose(decay_rows)
    step_cols = jnp.transpose(step[at])
    pair = 2 * dim
    first = lax.broadcasted_iota(jnp.int32, (length, pair), 1) < dim
    mixed = []
    for p in range(heads // 2):
        steps = jnp.where(
            first, step_cols[:, 2 * p : 2 * p + 1], step_cols[:, 2 * p + 1 : 2 * p + 2]
        )
        fed = x_act[:, p * pair : (p + 1) * pair] * steps
        fed_hi = fed.astype(BF16)
        fed_lo = (fed - fed_hi.astype(F32)).astype(BF16)
        fed_both = jnp.concatenate([fed_hi, fed_lo], axis=1)
        sums = []
        for h in (2 * p, 2 * p + 1):
            parts = []
            for lo, hi in ((0, half), (half, length)):
                gap = decay_cols[lo:hi, h : h + 1] - decay_rows[h : h + 1, :hi]
                weight = scores[lo:hi, :hi] * jnp.exp2(jnp.minimum(gap, 0.0))
                both = jnp.dot(weight.astype(BF16), fed_both[:hi], preferred_element_type=F32)
                parts.append(both[:, :pair] + both[:, pair:])
            sums.append(jnp.concatenate(parts, axis=0))
        mixed.append(jnp.where(first, sums[0], sums[1]))
    result = jnp.concatenate(mixed, axis=1) + w[5:6] * x_act
    out[0] = jnp.dot(pick[...], result.astype(BF16), preferred_element_type=F32).astype(BF16)


def one_hot(size, place):
    at = lax.broadcasted_iota(jnp.int32, (size, place.shape[1]), 0)
    return jnp.where(at == place, 1.0, 0.0).astype(BF16)


def one_hot_back(size, place):
    count = place.shape[1]
    column = jnp.transpose(jnp.broadcast_to(place.astype(F32), (8, count)))[:, :1]
    at = lax.broadcasted_iota(jnp.int32, (count, size), 1).astype(F32)
    return jnp.where(at == column, 1.0, 0.0).astype(BF16)


def chosen(pick, rows):
    return jnp.dot(pick, rows, preferred_element_type=F32).astype(BF16)


def loop(count, body):
    def step(i, carry):
        body(i)
        return carry

    lax.fori_loop(0, count, step, 0, unroll=2)


def pack_kernel(sc, rows, place, out):
    pick = one_hot(out.shape[1], place[sc[0]])

    def body(i):
        out[i] = chosen(pick, rows[:, i].reshape(place.shape[2], rows.shape[3]))

    loop(out.shape[0], body)


def widen_kernel(rows, place, out):
    def body(i):
        one = chosen(one_hot_back(rows.shape[1], place[i]), rows[i])
        out[i] = one.reshape(out.shape[1:])

    loop(out.shape[0], body)


def order_kernel(count, source, rows, place, out):
    def body(z):
        blocks = []
        for g in range(count):
            i = source[z * count + g]
            blocks.append(rows[i // count, i % count])
        out[z] = chosen(one_hot(out.shape[1], place[z]), jnp.concatenate(blocks, axis=0))

    loop(out.shape[0], body)


def unpack_kernel(sc, rows, place, out):
    pick = one_hot_back(rows.shape[1], place[sc[0]])

    def body(i):
        one = chosen(pick, rows[i])
        out[:, i] = one.reshape((out.shape[0],) + out.shape[2:])

    loop(rows.shape[0], body)


def finish_kernel(spread, sc, rows, own, oth):
    core, last, filled = sc[0], sc[1], sc[2]
    length, width = rows.shape[1:]
    half = length // 2
    keep = length // spread
    source = lax.broadcasted_iota(jnp.int32, (length, length), 1)
    index = lax.broadcasted_iota(jnp.int32, (length, length), 0)
    swapped = jnp.where(index < half, index + half, index - half)
    t = jnp.minimum(jnp.where(core == 0, index, swapped), last)
    place = (t % spread) * keep + t // spread
    pick = jnp.where((source == place) & (filled > 0), 1.0, 0.0).astype(BF16)

    def body(j):
        picked = chosen(pick, rows[j])
        at = pl.ds(pl.multiple_of(j * width, width), width)
        own[:, at] = picked[:half]
        oth[:, at] = picked[half:]

    loop(rows.shape[0], body)


def norm_kernel(sc, own, oth, gain, out):
    core = sc[0]
    width = own.shape[1]
    count = out.shape[0]
    here = pl.ds(pl.multiple_of(pl.program_id(0) * count, count), count)
    mine, other = own[here].astype(F32), oth[here].astype(F32)
    total = jnp.sum(mine * mine, axis=1, keepdims=True) + jnp.sum(
        other * other, axis=1, keepdims=True
    )
    scale = lax.rsqrt(total / (2 * width) + 1e-05)
    for values, side in ((mine, core), (other, 1 - core)):
        at = pl.ds(pl.multiple_of(side * width, width), width)
        out[:, at] = (values * scale * gain[:, at]).astype(BF16)


def grid_spec(scalars, grid, ins, outs, scratch=()):
    return pltpu.PrefetchScalarGridSpec(
        num_scalar_prefetch=scalars,
        grid=grid,
        in_specs=ins,
        out_specs=outs,
        scratch_shapes=list(scratch),
    )


def resident():
    return pl.BlockSpec(memory_space=pltpu.VMEM)


def once(kernel, scalars, outs, *operands, scratch=()):
    return pl.pallas_call(
        kernel,
        out_shape=outs,
        in_specs=[pl.BlockSpec(memory_space=pltpu.SMEM)] * scalars
        + [resident()] * (len(operands) - scalars),
        out_specs=jax.tree.map(lambda _: resident(), outs),
        scratch_shapes=list(scratch),
    )(*operands)


def per_device(
    x_in,
    bc_in,
    dt_in,
    dt_bias,
    a_log,
    skip_d,
    conv_x,
    conv_x_bias,
    conv_bc,
    conv_bc_bias,
    norm_gain,
    lengths,
    dest_group,
    dest_slot,
):
    n_ch = lax.axis_size("ch")
    n_grp = lax.axis_size("grp")
    n_z = n_ch // 2
    me = lax.axis_index("ch")
    my_group = lax.axis_index("grp")
    my_z, core = me // 2, me % 2
    half, channels = x_in.shape
    length = 2 * half
    mine = channels // 2
    width = channels // n_ch
    heads = a_log.shape[0]
    head_dim = width // heads
    head_half = dt_in.shape[1] // 2
    chunks = mine // width
    keep = length // n_z
    swap = [(i, i ^ 1) for i in range(n_ch)]
    rings = [[2 * z + c for z in range(n_z)] for c in range(2)]

    other_half = 1 - core
    x_oth = lax.ppermute(
        lax.dynamic_slice_in_dim(x_in, other_half * mine, mine, 1), "ch", swap
    )
    bc_oth = lax.ppermute(bc_in, "ch", swap)
    dt_oth = lax.ppermute(
        lax.dynamic_slice_in_dim(dt_in, other_half * head_half, head_half, 1), "ch", swap
    )
    shares = once(
        small_kernel,
        2,
        jax.ShapeDtypeStruct((n_z, 8, width), F32),
        skip_d,
        a_log,
        conv_x,
        conv_x_bias[None],
    )

    def exchange(a):
        return lax.all_to_all(
            a, "ch", split_axis=0, concat_axis=0, axis_index_groups=rings, tiled=True
        )

    by_chip = exchange(shares)
    pairs = n_grp * n_z
    ids = jnp.arange(pairs, dtype=jnp.int32)
    alive = dest_group >= 0
    units = jnp.where(alive, (jnp.minimum(lengths + 4, length) + n_z - 1) // n_z, 0)
    by_group = units.reshape(n_grp, n_z)
    ends = jnp.cumsum(by_group, axis=0)
    starts = ends - by_group
    target = jnp.where(alive, dest_group * n_z + dest_slot, pairs)
    match = target[None, :] == ids[:, None]

    def looked_up(values):
        return jnp.sum(jnp.where(match, values[None, :], 0), axis=1)

    to_units = looked_up(units).reshape(n_grp, n_z)
    slot_len = looked_up(lengths)
    source = looked_up((ids % n_z) * n_grp + ids // n_z)
    to_ends = jnp.cumsum(to_units, axis=0)
    to_starts = to_ends - to_units

    def places(count, start):
        k = jnp.arange(keep, dtype=jnp.int32)
        at = jnp.where(k < count.T[:, :, None], start.T[:, :, None] + k, -1)
        return at.reshape(n_z, 1, n_grp * keep)

    place_from = places(by_group, starts)
    place_to = places(to_units, to_starts)
    source = source.reshape(n_grp, n_z).T.reshape(-1)
    place_from, place_to, source = lax.optimization_barrier((place_from, place_to, source))
    z_only = my_z[None].astype(jnp.int32)

    my_dt = lax.dynamic_slice_in_dim(dt_in, core * head_half, head_half, 1)
    dt_both = jnp.concatenate(
        [jnp.where(core == 0, my_dt, dt_oth), jnp.where(core == 0, dt_oth, my_dt)], axis=0
    )
    used = lengths[my_group * n_z + my_z]
    valid = jnp.arange(length, dtype=jnp.int32) < used
    bias = lax.dynamic_slice_in_dim(dt_bias, core * head_half, head_half, 0)
    step = (
        jax.nn.softplus(dt_both.astype(F32) + bias[None, :]) * valid[:, None].astype(F32)
    ).astype(BF16).astype(F32)

    def by_chunk(a):
        a = a.reshape(chunks, heads, length)
        return jnp.pad(a, ((0, 0), (0, 8 - heads), (0, 0))).reshape(chunks * 8, length)

    step_t = by_chunk(step.T)
    wbc = jnp.concatenate([conv_bc, conv_bc_bias[None], jnp.zeros((3, conv_bc.shape[1]), F32)], axis=0)

    where_am_i = jnp.stack([core, used]).astype(jnp.int32)
    scores, summed, pick = once(
        functools.partial(prep_kernel, n_z),
        1,
        [
            jax.ShapeDtypeStruct((length, length), F32),
            jax.ShapeDtypeStruct(step_t.shape, F32),
            jax.ShapeDtypeStruct((length, length), BF16),
        ],
        where_am_i,
        bc_in,
        bc_oth,
        wbc,
        step_t,
        scratch=[pltpu.VMEM((2,) + bc_in.shape, BF16)],
    )
    by_chip, scores = lax.optimization_barrier((by_chip, scores))
    n_half = n_z // 2
    w_own = lax.dynamic_slice_in_dim(by_chip, core * n_half, n_half, 0)
    w_oth = lax.ppermute(
        lax.dynamic_slice_in_dim(by_chip, other_half * n_half, n_half, 0), "ch", swap
    )
    mixed = pl.pallas_call(
        functools.partial(mix_kernel, heads),
        out_shape=jax.ShapeDtypeStruct((chunks, length, width), BF16),
        grid_spec=grid_spec(
            1,
            (chunks,),
            [pl.BlockSpec((half, width), lambda j, sc: (0, sc[0] * chunks + j))]
            + [resident()] * 7,
            pl.BlockSpec((1, length, width), lambda j, sc: (j, 0, 0)),
            [pltpu.VMEM((2, half, width), BF16)],
        ),
        name="mix",
    )(where_am_i, x_in, x_oth, w_own, w_oth, step_t, scores, summed, pick)

    spread = lax.all_to_all(mixed, "grp", split_axis=0, concat_axis=0, tiled=True)

    full = n_grp * keep
    by_pair = (n_grp, n_z, keep, width)
    wide_shape = (n_z, n_grp, keep, width)

    def bf16(*shape):
        return jax.ShapeDtypeStruct(shape, BF16)

    def outward(size, spread):
        outgoing = once(
            pack_kernel, 1, bf16(n_z, size, width), z_only, spread.reshape(by_pair), place_from
        )
        return once(widen_kernel, 0, bf16(*wide_shape), exchange(outgoing), place_from)

    def homeward(size, wide):
        ordered = once(
            functools.partial(order_kernel, n_grp), 1, bf16(n_z, size, width), source, wide, place_to
        )
        landed = once(unpack_kernel, 1, bf16(*by_pair), z_only, exchange(ordered), place_to)
        return landed.reshape(n_grp, length, width)

    sizes = [s for s in LEVELS if s < full] + [full]

    def sized(step, needed, rows):
        level = jnp.sum((jnp.max(needed) > jnp.array(sizes[:-1], jnp.int32)).astype(jnp.int32))
        return lax.switch(level, [functools.partial(step, s) for s in sizes], rows)

    wide = sized(outward, ends[-1], spread)
    landed = sized(homeward, to_ends[-1], wide)
    rows = lax.all_to_all(landed, "grp", split_axis=0, concat_axis=0, tiled=True)

    slot = my_group * n_z + my_z
    last = jnp.minimum(slot_len[slot] + 3, length - 1)
    filled = jnp.any(target == slot)
    ends_at = jnp.stack([core, last, filled.astype(jnp.int32)]).astype(jnp.int32)
    own, oth = once(
        functools.partial(finish_kernel, n_z), 1, [bf16(half, mine)] * 2, ends_at, rows
    )
    got = lax.ppermute(oth, "ch", swap)
    step_rows = 32
    return pl.pallas_call(
        norm_kernel,
        out_shape=jax.ShapeDtypeStruct((half, channels), BF16),
        grid_spec=grid_spec(
            1,
            (half // step_rows,),
            [resident()] * 3,
            pl.BlockSpec((step_rows, channels), lambda i, sc: (i, 0)),
        ),
        name="norm",
    )(ends_at, own, got, norm_gain[None])


def solution(mesh):
    placed = (
        P(("grp", "ch"), None),
        P(("grp", "ch"), None),
        P(("grp", "ch"), None),
        P(),
        P("ch"),
        P("ch"),
        P(None, "ch"),
        P("ch"),
        P(),
        P(),
        P(),
        P(),
        P(),
        P(),
    )
    return jax.shard_map(
        per_device, mesh=mesh, in_specs=placed, out_specs=P(("grp", "ch"), None), check_vma=False
    )
```

```python
import functools

import jax
import jax.numpy as jnp
from jax import lax
from jax.experimental import pallas as pl
from jax.experimental.pallas import tpu as pltpu
from jax.sharding import PartitionSpec as P

LEVELS = (128, 152, 160, 168, 176, 184, 192, 200, 216)
LOG2E = 1.4426950408889634
F32 = jnp.float32
BF16 = jnp.bfloat16


def conv_silu(values, taps, bias, rows):
    count = 4
    total = jnp.broadcast_to(bias, values.shape)
    for k in range(count):
        back = count - 1 - k
        moved = values
        if back:
            moved = pltpu.roll(values, back, 0)
            top = jnp.where(rows[:8] >= back, moved[:8], 0.0)
            moved = jnp.concatenate([top, moved[8:]], axis=0)
        total = total + taps[k : k + 1] * moved
    low = 0.5 * total
    return low + low * jnp.tanh(low)


def small_kernel(skip, rate, taps, bias, out):
    count, width = out.shape[0], out.shape[2]
    heads = skip.shape[0]
    lane = lax.broadcasted_iota(jnp.int32, (1, width), 1)

    def by_channel(values):
        spread = jnp.full((1, width), values[0], F32)
        for h in range(1, heads):
            spread = jnp.where(lane >= h * (width // heads), values[h], spread)
        return spread

    rows = [taps[...], bias[...], by_channel(skip), by_channel(rate), jnp.zeros((1, width), F32)]
    share = jnp.concatenate(rows, axis=0)
    for i in range(count):
        out[i] = share


def joined(core, used, own, oth, buffer):
    buffer[core] = own
    buffer[1 - core] = oth
    both = buffer[...].reshape(2 * own.shape[0], own.shape[1]).astype(F32)
    rows = lax.broadcasted_iota(jnp.int32, both.shape, 0)
    return jnp.where(rows < used, both, 0.0), rows


def prep_kernel(spread, sc, bc_own, bc_oth, wbc, step, scores, summed, pick, buffer):
    bc, rows = joined(sc[0], sc[1], bc_own[...], bc_oth[...], buffer)
    length = bc.shape[0]
    act = conv_silu(bc, wbc[0:4], wbc[4:5], rows)
    state = act.shape[1] // 2
    later = lax.broadcasted_iota(jnp.int32, (length, length), 0)
    earlier = lax.broadcasted_iota(jnp.int32, (length, length), 1)
    raw = lax.dot_general(
        act[:, state:],
        act[:, :state],
        (((1,), (1,)), ((), ())),
        precision=lax.Precision.HIGHEST,
        preferred_element_type=F32,
    )
    scores[...] = jnp.where(later >= earlier, raw, 0.0)
    upper = jnp.where(later <= earlier, 1.0, 0.0).astype(F32)
    summed[...] = LOG2E * jnp.dot(
        step[...], upper, precision=lax.Precision.HIGHEST, preferred_element_type=F32
    )
    keep = length // spread
    place = (later % keep) * spread + later // keep
    pick[...] = jnp.where(earlier == place, 1.0, 0.0).astype(BF16)


def mix_kernel(
    heads, sc, x_own, x_oth, w_own, w_oth, step, scores, summed, pick, out, joint
):
    core, used = sc[0], sc[1]
    j = pl.program_id(0)
    half, both_width = x_own.shape
    columns = pl.ds(pl.multiple_of(j * both_width, both_width), both_width)
    x_two, rows_two = joined(core, used, x_own[...], x_oth[:, columns], joint)
    width = both_width // 2
    length = 2 * half
    dim = width // heads
    pair = 2 * dim
    first = lax.broadcasted_iota(jnp.int32, (length, pair), 1) < dim
    for q in range(2):
        x, rows = x_two[:, q * width : (q + 1) * width], rows_two[:, :width]
        w = jnp.where(core == q, w_own[j], w_oth[j])
        x_act = conv_silu(x, w[0:4], w[4:5], rows)
        at = pl.ds(pl.multiple_of(16 * j + 8 * q, 8), 8)
        rates = -jnp.exp(w[6:7])
        sums_here = summed[at]
        scaled = [sums_here[h : h + 1] * rates[:, h * dim : h * dim + 1] for h in range(heads)]
        decay_rows = jnp.concatenate(scaled + [sums_here[heads:]], axis=0)
        decay_cols = jnp.transpose(decay_rows)
        step_cols = jnp.transpose(step[at])
        mixed = []
        for p in range(heads // 2):
            steps = jnp.where(
                first, step_cols[:, 2 * p : 2 * p + 1], step_cols[:, 2 * p + 1 : 2 * p + 2]
            )
            fed = x_act[:, p * pair : (p + 1) * pair] * steps
            fed_hi = fed.astype(BF16)
            fed_lo = (fed - fed_hi.astype(F32)).astype(BF16)
            fed_both = jnp.concatenate([fed_hi, fed_lo], axis=1)
            sums = []
            for h in (2 * p, 2 * p + 1):
                parts = []
                for lo, hi in ((0, half), (half, length)):
                    gap = decay_cols[lo:hi, h : h + 1] - decay_rows[h : h + 1, :hi]
                    weight = scores[lo:hi, :hi] * jnp.exp2(jnp.minimum(gap, 0.0))
                    both = jnp.dot(
                        weight.astype(BF16), fed_both[:hi], preferred_element_type=F32
                    )
                    parts.append(both[:, :pair] + both[:, pair:])
                sums.append(jnp.concatenate(parts, axis=0))
            mixed.append(jnp.where(first, sums[0], sums[1]))
        result = jnp.concatenate(mixed, axis=1) + w[5:6] * x_act
        out[q] = jnp.dot(
            pick[...], result.astype(BF16), preferred_element_type=F32
        ).astype(BF16)


def one_hot(size, place):
    at = lax.broadcasted_iota(jnp.int32, (size, place.shape[1]), 0)
    return jnp.where(at == place, 1.0, 0.0).astype(BF16)


def one_hot_back(size, place):
    count = place.shape[1]
    column = jnp.transpose(jnp.broadcast_to(place.astype(F32), (8, count)))[:, :1]
    at = lax.broadcasted_iota(jnp.int32, (count, size), 1).astype(F32)
    return jnp.where(at == column, 1.0, 0.0).astype(BF16)


def chosen(pick, rows):
    return jnp.dot(pick, rows, preferred_element_type=F32).astype(BF16)


def loop(count, body):
    def step(i, carry):
        body(i)
        return carry

    lax.fori_loop(0, count, step, 0, unroll=2)


def pack_kernel(sc, rows, place, out):
    pick = one_hot(out.shape[1], place[sc[0]])

    def body(i):
        out[i] = chosen(pick, rows[:, i].reshape(place.shape[2], rows.shape[3]))

    loop(out.shape[0], body)


def widen_kernel(rows, place, out):
    def body(i):
        one = chosen(one_hot_back(rows.shape[1], place[i]), rows[i])
        out[i] = one.reshape(out.shape[1:])

    loop(out.shape[0], body)


def order_kernel(count, source, rows, place, out):
    def body(z):
        blocks = []
        for g in range(count):
            i = source[z * count + g]
            blocks.append(rows[i // count, i % count])
        out[z] = chosen(one_hot(out.shape[1], place[z]), jnp.concatenate(blocks, axis=0))

    loop(out.shape[0], body)


def unpack_kernel(sc, rows, place, out):
    pick = one_hot_back(rows.shape[1], place[sc[0]])

    def body(i):
        one = chosen(pick, rows[i])
        out[:, i] = one.reshape((out.shape[0],) + out.shape[2:])

    loop(rows.shape[0], body)


def finish_kernel(spread, sc, rows, own, oth):
    core, last, filled = sc[0], sc[1], sc[2]
    length, width = rows.shape[1:]
    half = length // 2
    keep = length // spread
    source = lax.broadcasted_iota(jnp.int32, (length, length), 1)
    index = lax.broadcasted_iota(jnp.int32, (length, length), 0)
    swapped = jnp.where(index < half, index + half, index - half)
    t = jnp.minimum(jnp.where(core == 0, index, swapped), last)
    place = (t % spread) * keep + t // spread
    pick = jnp.where((source == place) & (filled > 0), 1.0, 0.0).astype(BF16)

    def body(j):
        picked = chosen(pick, rows[j])
        at = pl.ds(pl.multiple_of(j * width, width), width)
        own[:, at] = picked[:half]
        oth[:, at] = picked[half:]

    loop(rows.shape[0], body)


def norm_kernel(sc, own, oth, gain, out):
    core = sc[0]
    width = own.shape[1]
    count = out.shape[0]
    here = pl.ds(pl.multiple_of(pl.program_id(0) * count, count), count)
    mine, other = own[here].astype(F32), oth[here].astype(F32)
    total = jnp.sum(mine * mine, axis=1, keepdims=True) + jnp.sum(
        other * other, axis=1, keepdims=True
    )
    scale = lax.rsqrt(total / (2 * width) + 1e-05)
    for values, side in ((mine, core), (other, 1 - core)):
        at = pl.ds(pl.multiple_of(side * width, width), width)
        out[:, at] = (values * scale * gain[:, at]).astype(BF16)


def grid_spec(scalars, grid, ins, outs, scratch=()):
    return pltpu.PrefetchScalarGridSpec(
        num_scalar_prefetch=scalars,
        grid=grid,
        in_specs=ins,
        out_specs=outs,
        scratch_shapes=list(scratch),
    )


def resident():
    return pl.BlockSpec(memory_space=pltpu.VMEM)


def limits():
    return pltpu.CompilerParams(vmem_limit_bytes=24 << 20)


def once(kernel, scalars, outs, *operands, scratch=()):
    return pl.pallas_call(
        kernel,
        out_shape=outs,
        in_specs=[pl.BlockSpec(memory_space=pltpu.SMEM)] * scalars
        + [resident()] * (len(operands) - scalars),
        out_specs=jax.tree.map(lambda _: resident(), outs),
        scratch_shapes=list(scratch),
        compiler_params=limits(),
    )(*operands)


def per_device(
    x_in,
    bc_in,
    dt_in,
    dt_bias,
    a_log,
    skip_d,
    conv_x,
    conv_x_bias,
    conv_bc,
    conv_bc_bias,
    norm_gain,
    lengths,
    dest_group,
    dest_slot,
):
    n_ch = lax.axis_size("ch")
    n_grp = lax.axis_size("grp")
    n_z = n_ch // 2
    me = lax.axis_index("ch")
    my_group = lax.axis_index("grp")
    my_z, core = me // 2, me % 2
    half, channels = x_in.shape
    length = 2 * half
    mine = channels // 2
    width = channels // n_ch
    heads = a_log.shape[0]
    head_dim = width // heads
    head_half = dt_in.shape[1] // 2
    chunks = mine // width
    keep = length // n_z
    swap = [(i, i ^ 1) for i in range(n_ch)]
    rings = [[2 * z + c for z in range(n_z)] for c in range(2)]

    other_half = 1 - core
    x_oth = lax.ppermute(
        lax.dynamic_slice_in_dim(x_in, other_half * mine, mine, 1), "ch", swap
    )
    bc_oth = lax.ppermute(bc_in, "ch", swap)
    dt_oth = lax.ppermute(
        lax.dynamic_slice_in_dim(dt_in, other_half * head_half, head_half, 1), "ch", swap
    )
    shares = once(
        small_kernel,
        2,
        jax.ShapeDtypeStruct((n_z, 8, width), F32),
        skip_d,
        a_log,
        conv_x,
        conv_x_bias[None],
    )

    def exchange(a):
        return lax.all_to_all(
            a, "ch", split_axis=0, concat_axis=0, axis_index_groups=rings, tiled=True
        )

    by_chip = exchange(shares)
    pairs = n_grp * n_z
    ids = jnp.arange(pairs, dtype=jnp.int32)
    alive = dest_group >= 0
    units = jnp.where(alive, (jnp.minimum(lengths + 4, length) + n_z - 1) // n_z, 0)
    by_group = units.reshape(n_grp, n_z)
    ends = jnp.cumsum(by_group, axis=0)
    starts = ends - by_group
    target = jnp.where(alive, dest_group * n_z + dest_slot, pairs)
    match = target[None, :] == ids[:, None]

    def looked_up(values):
        return jnp.sum(jnp.where(match, values[None, :], 0), axis=1)

    to_units = looked_up(units).reshape(n_grp, n_z)
    slot_len = looked_up(lengths)
    source = looked_up((ids % n_z) * n_grp + ids // n_z)
    to_ends = jnp.cumsum(to_units, axis=0)
    to_starts = to_ends - to_units

    def places(count, start):
        k = jnp.arange(keep, dtype=jnp.int32)
        at = jnp.where(k < count.T[:, :, None], start.T[:, :, None] + k, -1)
        return at.reshape(n_z, 1, n_grp * keep)

    place_from = places(by_group, starts)
    place_to = places(to_units, to_starts)
    source = source.reshape(n_grp, n_z).T.reshape(-1)
    place_from, place_to, source = lax.optimization_barrier((place_from, place_to, source))
    z_only = my_z[None].astype(jnp.int32)

    my_dt = lax.dynamic_slice_in_dim(dt_in, core * head_half, head_half, 1)
    dt_both = jnp.concatenate(
        [jnp.where(core == 0, my_dt, dt_oth), jnp.where(core == 0, dt_oth, my_dt)], axis=0
    )
    used = lengths[my_group * n_z + my_z]
    valid = jnp.arange(length, dtype=jnp.int32) < used
    bias = lax.dynamic_slice_in_dim(dt_bias, core * head_half, head_half, 0)
    step = (
        jax.nn.softplus(dt_both.astype(F32) + bias[None, :]) * valid[:, None].astype(F32)
    ).astype(BF16).astype(F32)

    def by_chunk(a):
        a = a.reshape(chunks, heads, length)
        return jnp.pad(a, ((0, 0), (0, 8 - heads), (0, 0))).reshape(chunks * 8, length)

    step_t = by_chunk(step.T)
    wbc = jnp.concatenate([conv_bc, conv_bc_bias[None], jnp.zeros((3, conv_bc.shape[1]), F32)], axis=0)

    where_am_i = jnp.stack([core, used]).astype(jnp.int32)
    scores, summed, pick = once(
        functools.partial(prep_kernel, n_z),
        1,
        [
            jax.ShapeDtypeStruct((length, length), F32),
            jax.ShapeDtypeStruct(step_t.shape, F32),
            jax.ShapeDtypeStruct((length, length), BF16),
        ],
        where_am_i,
        bc_in,
        bc_oth,
        wbc,
        step_t,
        scratch=[pltpu.VMEM((2,) + bc_in.shape, BF16)],
    )
    by_chip, scores = lax.optimization_barrier((by_chip, scores))
    n_half = n_z // 2
    w_own = lax.dynamic_slice_in_dim(by_chip, core * n_half, n_half, 0)
    w_oth = lax.ppermute(
        lax.dynamic_slice_in_dim(by_chip, other_half * n_half, n_half, 0), "ch", swap
    )
    mixed = pl.pallas_call(
        functools.partial(mix_kernel, heads),
        out_shape=jax.ShapeDtypeStruct((chunks, length, width), BF16),
        grid_spec=grid_spec(
            1,
            (chunks // 2,),
            [pl.BlockSpec((half, 2 * width), lambda j, sc: (0, sc[0] * (chunks // 2) + j))]
            + [resident()] * 7,
            pl.BlockSpec((2, length, width), lambda j, sc: (j, 0, 0)),
            [pltpu.VMEM((2, half, 2 * width), BF16)],
        ),
        compiler_params=limits(),
        name="mix",
    )(where_am_i, x_in, x_oth, w_own, w_oth, step_t, scores, summed, pick)

    spread = lax.all_to_all(mixed, "grp", split_axis=0, concat_axis=0, tiled=True)

    full = n_grp * keep
    by_pair = (n_grp, n_z, keep, width)
    wide_shape = (n_z, n_grp, keep, width)

    def bf16(*shape):
        return jax.ShapeDtypeStruct(shape, BF16)

    def outward(size, spread):
        outgoing = once(
            pack_kernel, 1, bf16(n_z, size, width), z_only, spread.reshape(by_pair), place_from
        )
        return once(widen_kernel, 0, bf16(*wide_shape), exchange(outgoing), place_from)

    def homeward(size, wide):
        ordered = once(
            functools.partial(order_kernel, n_grp), 1, bf16(n_z, size, width), source, wide, place_to
        )
        landed = once(unpack_kernel, 1, bf16(*by_pair), z_only, exchange(ordered), place_to)
        return landed.reshape(n_grp, length, width)

    sizes = [s for s in LEVELS if s < full] + [full]

    def sized(step, needed, rows):
        level = jnp.sum((jnp.max(needed) > jnp.array(sizes[:-1], jnp.int32)).astype(jnp.int32))
        return lax.switch(level, [functools.partial(step, s) for s in sizes], rows)

    wide = sized(outward, ends[-1], spread)
    landed = sized(homeward, to_ends[-1], wide)
    rows = lax.all_to_all(landed, "grp", split_axis=0, concat_axis=0, tiled=True)

    slot = my_group * n_z + my_z
    last = jnp.minimum(slot_len[slot] + 3, length - 1)
    filled = jnp.any(target == slot)
    ends_at = jnp.stack([core, last, filled.astype(jnp.int32)]).astype(jnp.int32)
    own, oth = once(
        functools.partial(finish_kernel, n_z), 1, [bf16(half, mine)] * 2, ends_at, rows
    )
    got = lax.ppermute(oth, "ch", swap)
    step_rows = 32
    return pl.pallas_call(
        norm_kernel,
        out_shape=jax.ShapeDtypeStruct((half, channels), BF16),
        grid_spec=grid_spec(
            1,
            (half // step_rows,),
            [resident()] * 3,
            pl.BlockSpec((step_rows, channels), lambda i, sc: (i, 0)),
        ),
        compiler_params=limits(),
        name="norm",
    )(ends_at, own, got, norm_gain[None])


def solution(mesh):
    placed = (
        P(("grp", "ch"), None),
        P(("grp", "ch"), None),
        P(("grp", "ch"), None),
        P(),
        P("ch"),
        P("ch"),
        P(None, "ch"),
        P("ch"),
        P(),
        P(),
        P(),
        P(),
        P(),
        P(),
    )
    return jax.shard_map(
        per_device, mesh=mesh, in_specs=placed, out_specs=P(("grp", "ch"), None), check_vma=False
    )
```

```python
import functools

import jax
import jax.numpy as jnp
from jax import lax
from jax.experimental import pallas as pl
from jax.experimental.pallas import tpu as pltpu
from jax.sharding import PartitionSpec as P

LEVELS = (128, 152, 160, 168, 176, 184, 192, 200, 216)
LOG2E = 1.4426950408889634
F32 = jnp.float32
BF16 = jnp.bfloat16


def conv_silu(values, taps, bias, rows):
    count = 4
    total = jnp.broadcast_to(bias, values.shape)
    for k in range(count):
        back = count - 1 - k
        moved = values
        if back:
            moved = pltpu.roll(values, back, 0)
            top = jnp.where(rows[:8] >= back, moved[:8], 0.0)
            moved = jnp.concatenate([top, moved[8:]], axis=0)
        total = total + taps[k : k + 1] * moved
    low = 0.5 * total
    return low + low * jnp.tanh(low)


def small_kernel(skip, rate, taps, bias, out):
    width = out.shape[1]
    heads = skip.shape[0]
    lane = lax.broadcasted_iota(jnp.int32, (1, width), 1)

    def by_channel(values):
        spread = jnp.full((1, width), values[0], F32)
        for h in range(1, heads):
            spread = jnp.where(lane >= h * (width // heads), values[h], spread)
        return spread

    rows = [taps[...], bias[...], by_channel(skip), by_channel(rate), jnp.zeros((1, width), F32)]
    out[...] = jnp.concatenate(rows, axis=0)


def joined(core, used, own, oth, buffer):
    buffer[core] = own
    buffer[1 - core] = oth
    both = buffer[...].reshape(2 * own.shape[0], own.shape[1]).astype(F32)
    rows = lax.broadcasted_iota(jnp.int32, both.shape, 0)
    return jnp.where(rows < used, both, 0.0), rows


def prep_kernel(spread, sc, bc_own, bc_oth, wbc, step, scores, summed, pick, buffer):
    bc, rows = joined(sc[0], sc[1], bc_own[...], bc_oth[...], buffer)
    length = bc.shape[0]
    act = conv_silu(bc, wbc[0:4], wbc[4:5], rows)
    state = act.shape[1] // 2
    later = lax.broadcasted_iota(jnp.int32, (length, length), 0)
    earlier = lax.broadcasted_iota(jnp.int32, (length, length), 1)
    raw = lax.dot_general(
        act[:, state:],
        act[:, :state],
        (((1,), (1,)), ((), ())),
        precision=lax.Precision.HIGHEST,
        preferred_element_type=F32,
    )
    scores[...] = jnp.where(later >= earlier, raw, 0.0)
    upper = jnp.where(later <= earlier, 1.0, 0.0).astype(F32)
    summed[...] = LOG2E * jnp.dot(
        step[...], upper, precision=lax.Precision.HIGHEST, preferred_element_type=F32
    )
    keep = length // spread
    place = (later % keep) * spread + later // keep
    pick[...] = jnp.where(earlier == place, 1.0, 0.0).astype(BF16)


def mix_kernel(
    heads, sc, x_own, x_oth, w_half, step, scores, summed, pick, out, joint
):
    core, used = sc[0], sc[1]
    j = pl.program_id(0)
    half, both_width = x_own.shape
    columns = pl.ds(pl.multiple_of(j * both_width, both_width), both_width)
    x_two, rows_two = joined(core, used, x_own[...], x_oth[:, columns], joint)
    width = both_width // 2
    length = 2 * half
    dim = width // heads
    pair = 2 * dim
    first = lax.broadcasted_iota(jnp.int32, (length, pair), 1) < dim
    for q in range(2):
        x, rows = x_two[:, q * width : (q + 1) * width], rows_two[:, :width]
        w = w_half[2 * j + q]
        x_act = conv_silu(x, w[0:4], w[4:5], rows)
        at = pl.ds(pl.multiple_of(16 * j + 8 * q, 8), 8)
        rates = -jnp.exp(w[6:7])
        sums_here = summed[at]
        scaled = [sums_here[h : h + 1] * rates[:, h * dim : h * dim + 1] for h in range(heads)]
        decay_rows = jnp.concatenate(scaled + [sums_here[heads:]], axis=0)
        decay_cols = jnp.transpose(decay_rows)
        step_cols = jnp.transpose(step[at])
        mixed = []
        for p in range(heads // 2):
            steps = jnp.where(
                first, step_cols[:, 2 * p : 2 * p + 1], step_cols[:, 2 * p + 1 : 2 * p + 2]
            )
            fed = x_act[:, p * pair : (p + 1) * pair] * steps
            fed_hi = fed.astype(BF16)
            fed_lo = (fed - fed_hi.astype(F32)).astype(BF16)
            fed_both = jnp.concatenate([fed_hi, fed_lo], axis=1)
            sums = []
            for h in (2 * p, 2 * p + 1):
                parts = []
                for lo, hi in ((0, half), (half, length)):
                    gap = decay_cols[lo:hi, h : h + 1] - decay_rows[h : h + 1, :hi]
                    weight = scores[lo:hi, :hi] * jnp.exp2(jnp.minimum(gap, 0.0))
                    both = jnp.dot(
                        weight.astype(BF16), fed_both[:hi], preferred_element_type=F32
                    )
                    parts.append(both[:, :pair] + both[:, pair:])
                sums.append(jnp.concatenate(parts, axis=0))
            mixed.append(jnp.where(first, sums[0], sums[1]))
        result = jnp.concatenate(mixed, axis=1) + w[5:6] * x_act
        out[q] = jnp.dot(
            pick[...], result.astype(BF16), preferred_element_type=F32
        ).astype(BF16)


def one_hot(size, place):
    at = lax.broadcasted_iota(jnp.int32, (size, place.shape[1]), 0)
    return jnp.where(at == place, 1.0, 0.0).astype(BF16)


def one_hot_back(size, place):
    count = place.shape[1]
    column = jnp.transpose(jnp.broadcast_to(place.astype(F32), (8, count)))[:, :1]
    at = lax.broadcasted_iota(jnp.int32, (count, size), 1).astype(F32)
    return jnp.where(at == column, 1.0, 0.0).astype(BF16)


def chosen(pick, rows):
    return jnp.dot(pick, rows, preferred_element_type=F32).astype(BF16)


def loop(count, body):
    def step(i, carry):
        body(i)
        return carry

    lax.fori_loop(0, count, step, 0, unroll=2)


def pack_kernel(sc, rows, place, out):
    pick = one_hot(out.shape[1], place[sc[0]])

    def body(i):
        out[i] = chosen(pick, rows[:, i].reshape(place.shape[2], rows.shape[3]))

    loop(out.shape[0], body)


def widen_kernel(rows, place, out):
    def body(i):
        one = chosen(one_hot_back(rows.shape[1], place[i]), rows[i])
        out[i] = one.reshape(out.shape[1:])

    loop(out.shape[0], body)


def order_kernel(count, source, rows, place, out):
    def body(z):
        blocks = []
        for g in range(count):
            i = source[z * count + g]
            blocks.append(rows[i // count, i % count])
        out[z] = chosen(one_hot(out.shape[1], place[z]), jnp.concatenate(blocks, axis=0))

    loop(out.shape[0], body)


def unpack_kernel(sc, rows, place, out):
    pick = one_hot_back(rows.shape[1], place[sc[0]])

    def body(i):
        one = chosen(pick, rows[i])
        out[:, i] = one.reshape((out.shape[0],) + out.shape[2:])

    loop(rows.shape[0], body)


def finish_kernel(spread, sc, rows, own, oth):
    core, last, filled = sc[0], sc[1], sc[2]
    length, width = rows.shape[1:]
    half = length // 2
    keep = length // spread
    source = lax.broadcasted_iota(jnp.int32, (length, length), 1)
    index = lax.broadcasted_iota(jnp.int32, (length, length), 0)
    swapped = jnp.where(index < half, index + half, index - half)
    t = jnp.minimum(jnp.where(core == 0, index, swapped), last)
    place = (t % spread) * keep + t // spread
    pick = jnp.where((source == place) & (filled > 0), 1.0, 0.0).astype(BF16)

    def body(j):
        picked = chosen(pick, rows[j])
        at = pl.ds(pl.multiple_of(j * width, width), width)
        own[:, at] = picked[:half]
        oth[:, at] = picked[half:]

    loop(rows.shape[0], body)


def norm_kernel(sc, own, oth, gain, out):
    core = sc[0]
    width = own.shape[1]
    count = out.shape[0]
    here = pl.ds(pl.multiple_of(pl.program_id(0) * count, count), count)
    mine, other = own[here].astype(F32), oth[here].astype(F32)
    total = jnp.sum(mine * mine, axis=1, keepdims=True) + jnp.sum(
        other * other, axis=1, keepdims=True
    )
    scale = lax.rsqrt(total / (2 * width) + 1e-05)
    for values, side in ((mine, core), (other, 1 - core)):
        at = pl.ds(pl.multiple_of(side * width, width), width)
        out[:, at] = (values * scale * gain[:, at]).astype(BF16)


def grid_spec(scalars, grid, ins, outs, scratch=()):
    return pltpu.PrefetchScalarGridSpec(
        num_scalar_prefetch=scalars,
        grid=grid,
        in_specs=ins,
        out_specs=outs,
        scratch_shapes=list(scratch),
    )


def resident():
    return pl.BlockSpec(memory_space=pltpu.VMEM)


def limits():
    return pltpu.CompilerParams(vmem_limit_bytes=24 << 20)


def once(kernel, scalars, outs, *operands, scratch=(), params=None):
    return pl.pallas_call(
        kernel,
        out_shape=outs,
        in_specs=[pl.BlockSpec(memory_space=pltpu.SMEM)] * scalars
        + [resident()] * (len(operands) - scalars),
        out_specs=jax.tree.map(lambda _: resident(), outs),
        scratch_shapes=list(scratch),
        compiler_params=params or limits(),
    )(*operands)


def per_device(
    x_in,
    bc_in,
    dt_in,
    dt_bias,
    a_log,
    skip_d,
    conv_x,
    conv_x_bias,
    conv_bc,
    conv_bc_bias,
    norm_gain,
    lengths,
    dest_group,
    dest_slot,
):
    n_ch = lax.axis_size("ch")
    n_grp = lax.axis_size("grp")
    n_z = n_ch // 2
    me = lax.axis_index("ch")
    my_group = lax.axis_index("grp")
    my_z, core = me // 2, me % 2
    half, channels = x_in.shape
    length = 2 * half
    mine = channels // 2
    width = channels // n_ch
    heads = a_log.shape[0]
    head_dim = width // heads
    head_half = dt_in.shape[1] // 2
    chunks = mine // width
    keep = length // n_z
    swap = [(i, i ^ 1) for i in range(n_ch)]
    rings = [[2 * z + c for z in range(n_z)] for c in range(2)]

    other_half = 1 - core
    x_oth = lax.ppermute(
        lax.dynamic_slice_in_dim(x_in, other_half * mine, mine, 1), "ch", swap
    )
    bc_oth = lax.ppermute(bc_in, "ch", swap)
    dt_oth = lax.ppermute(
        lax.dynamic_slice_in_dim(dt_in, other_half * head_half, head_half, 1), "ch", swap
    )
    share = once(
        small_kernel,
        2,
        jax.ShapeDtypeStruct((8, width), F32),
        skip_d,
        a_log,
        conv_x,
        conv_x_bias[None],
        params=pltpu.CompilerParams(),
    )
    to_half = [(i, 2 * (i % n_z) + i // n_z) for i in range(n_ch)]
    share = lax.ppermute(share, "ch", to_half)

    def exchange(a):
        return lax.all_to_all(
            a, "ch", split_axis=0, concat_axis=0, axis_index_groups=rings, tiled=True
        )

    w_half = exchange(jnp.broadcast_to(share[None], (n_z, 8, width)))
    pairs = n_grp * n_z
    ids = jnp.arange(pairs, dtype=jnp.int32)
    alive = dest_group >= 0
    units = jnp.where(alive, (jnp.minimum(lengths + 4, length) + n_z - 1) // n_z, 0)
    by_group = units.reshape(n_grp, n_z)
    ends = jnp.cumsum(by_group, axis=0)
    starts = ends - by_group
    target = jnp.where(alive, dest_group * n_z + dest_slot, pairs)
    match = target[None, :] == ids[:, None]

    def looked_up(values):
        return jnp.sum(jnp.where(match, values[None, :], 0), axis=1)

    to_units = looked_up(units).reshape(n_grp, n_z)
    slot_len = looked_up(lengths)
    source = looked_up((ids % n_z) * n_grp + ids // n_z)
    to_ends = jnp.cumsum(to_units, axis=0)
    to_starts = to_ends - to_units

    def places(count, start):
        k = jnp.arange(keep, dtype=jnp.int32)
        at = jnp.where(k < count.T[:, :, None], start.T[:, :, None] + k, -1)
        return at.reshape(n_z, 1, n_grp * keep)

    place_from = places(by_group, starts)
    place_to = places(to_units, to_starts)
    source = source.reshape(n_grp, n_z).T.reshape(-1)
    place_from, place_to, source = lax.optimization_barrier((place_from, place_to, source))
    z_only = my_z[None].astype(jnp.int32)

    my_dt = lax.dynamic_slice_in_dim(dt_in, core * head_half, head_half, 1)
    dt_both = jnp.concatenate(
        [jnp.where(core == 0, my_dt, dt_oth), jnp.where(core == 0, dt_oth, my_dt)], axis=0
    )
    used = lengths[my_group * n_z + my_z]
    valid = jnp.arange(length, dtype=jnp.int32) < used
    bias = lax.dynamic_slice_in_dim(dt_bias, core * head_half, head_half, 0)
    step = (
        jax.nn.softplus(dt_both.astype(F32) + bias[None, :]) * valid[:, None].astype(F32)
    ).astype(BF16).astype(F32)

    def by_chunk(a):
        a = a.reshape(chunks, heads, length)
        return jnp.pad(a, ((0, 0), (0, 8 - heads), (0, 0))).reshape(chunks * 8, length)

    step_t = by_chunk(step.T)
    wbc = jnp.concatenate([conv_bc, conv_bc_bias[None], jnp.zeros((3, conv_bc.shape[1]), F32)], axis=0)

    where_am_i = jnp.stack([core, used]).astype(jnp.int32)
    scores, summed, pick = once(
        functools.partial(prep_kernel, n_z),
        1,
        [
            jax.ShapeDtypeStruct((length, length), F32),
            jax.ShapeDtypeStruct(step_t.shape, F32),
            jax.ShapeDtypeStruct((length, length), BF16),
        ],
        where_am_i,
        bc_in,
        bc_oth,
        wbc,
        step_t,
        scratch=[pltpu.VMEM((2,) + bc_in.shape, BF16)],
        params=pltpu.CompilerParams(),
    )
    w_half, scores = lax.optimization_barrier((w_half, scores))
    mixed = pl.pallas_call(
        functools.partial(mix_kernel, heads),
        out_shape=jax.ShapeDtypeStruct((chunks, length, width), BF16),
        grid_spec=grid_spec(
            1,
            (chunks // 2,),
            [pl.BlockSpec((half, 2 * width), lambda j, sc: (0, sc[0] * (chunks // 2) + j))]
            + [resident()] * 6,
            pl.BlockSpec((2, length, width), lambda j, sc: (j, 0, 0)),
            [pltpu.VMEM((2, half, 2 * width), BF16)],
        ),
        name="mix",
    )(where_am_i, x_in, x_oth, w_half, step_t, scores, summed, pick)

    spread = lax.all_to_all(mixed, "grp", split_axis=0, concat_axis=0, tiled=True)

    full = n_grp * keep
    by_pair = (n_grp, n_z, keep, width)
    wide_shape = (n_z, n_grp, keep, width)

    def bf16(*shape):
        return jax.ShapeDtypeStruct(shape, BF16)

    def outward(size, spread):
        outgoing = once(
            pack_kernel, 1, bf16(n_z, size, width), z_only, spread.reshape(by_pair), place_from
        )
        return once(widen_kernel, 0, bf16(*wide_shape), exchange(outgoing), place_from)

    def homeward(size, wide):
        ordered = once(
            functools.partial(order_kernel, n_grp), 1, bf16(n_z, size, width), source, wide, place_to
        )
        landed = once(unpack_kernel, 1, bf16(*by_pair), z_only, exchange(ordered), place_to)
        return landed.reshape(n_grp, length, width)

    sizes = [s for s in LEVELS if s < full] + [full]

    def sized(step, needed, rows):
        level = jnp.sum((jnp.max(needed) > jnp.array(sizes[:-1], jnp.int32)).astype(jnp.int32))
        return lax.switch(level, [functools.partial(step, s) for s in sizes], rows)

    wide = sized(outward, ends[-1], spread)
    landed = sized(homeward, to_ends[-1], wide)
    rows = lax.all_to_all(landed, "grp", split_axis=0, concat_axis=0, tiled=True)

    slot = my_group * n_z + my_z
    last = jnp.minimum(slot_len[slot] + 3, length - 1)
    filled = jnp.any(target == slot)
    ends_at = jnp.stack([core, last, filled.astype(jnp.int32)]).astype(jnp.int32)
    own, oth = once(
        functools.partial(finish_kernel, n_z), 1, [bf16(half, mine)] * 2, ends_at, rows
    )
    got = lax.ppermute(oth, "ch", swap)
    step_rows = 32
    return pl.pallas_call(
        norm_kernel,
        out_shape=jax.ShapeDtypeStruct((half, channels), BF16),
        grid_spec=grid_spec(
            1,
            (half // step_rows,),
            [resident()] * 3,
            pl.BlockSpec((step_rows, channels), lambda i, sc: (i, 0)),
        ),
        compiler_params=limits(),
        name="norm",
    )(ends_at, own, got, norm_gain[None])


def solution(mesh):
    placed = (
        P(("grp", "ch"), None),
        P(("grp", "ch"), None),
        P(("grp", "ch"), None),
        P(),
        P("ch"),
        P("ch"),
        P(None, "ch"),
        P("ch"),
        P(),
        P(),
        P(),
        P(),
        P(),
        P(),
    )
    return jax.shard_map(
        per_device, mesh=mesh, in_specs=placed, out_specs=P(("grp", "ch"), None), check_vma=False
    )
```

```python
import functools

import jax
import jax.numpy as jnp
from jax import lax
from jax.experimental import pallas as pl
from jax.experimental.pallas import tpu as pltpu
from jax.sharding import PartitionSpec as P

LEVELS = (128, 152, 160, 168, 176, 184, 192, 200, 216)
LOG2E = 1.4426950408889634
F32 = jnp.float32
BF16 = jnp.bfloat16


def conv_silu(values, taps, bias, rows):
    count = 4
    total = jnp.broadcast_to(bias, values.shape)
    for k in range(count):
        back = count - 1 - k
        moved = values
        if back:
            moved = pltpu.roll(values, back, 0)
            top = jnp.where(rows[:8] >= back, moved[:8], 0.0)
            moved = jnp.concatenate([top, moved[8:]], axis=0)
        total = total + taps[k : k + 1] * moved
    low = 0.5 * total
    return low + low * jnp.tanh(low)


def small_kernel(skip, rate, taps, bias, out):
    count, width = out.shape[0], out.shape[2]
    heads = skip.shape[0]
    lane = lax.broadcasted_iota(jnp.int32, (1, width), 1)

    def by_channel(values):
        spread = jnp.full((1, width), values[0], F32)
        for h in range(1, heads):
            spread = jnp.where(lane >= h * (width // heads), values[h], spread)
        return spread

    rows = [taps[...], bias[...], by_channel(skip), by_channel(rate), jnp.zeros((1, width), F32)]
    share = jnp.concatenate(rows, axis=0)
    for i in range(count):
        out[i] = share


def joined(core, used, own, oth, buffer):
    buffer[core] = own
    buffer[1 - core] = oth
    both = buffer[...].reshape(2 * own.shape[0], own.shape[1]).astype(F32)
    rows = lax.broadcasted_iota(jnp.int32, both.shape, 0)
    return jnp.where(rows < used, both, 0.0), rows


def prep_kernel(spread, sc, bc_own, bc_oth, wbc, step, scores, summed, pick, buffer):
    bc, rows = joined(sc[0], sc[1], bc_own[...], bc_oth[...], buffer)
    length = bc.shape[0]
    act = conv_silu(bc, wbc[0:4], wbc[4:5], rows)
    state = act.shape[1] // 2
    later = lax.broadcasted_iota(jnp.int32, (length, length), 0)
    earlier = lax.broadcasted_iota(jnp.int32, (length, length), 1)
    raw = lax.dot_general(
        act[:, state:],
        act[:, :state],
        (((1,), (1,)), ((), ())),
        precision=lax.Precision.HIGHEST,
        preferred_element_type=F32,
    )
    scores[...] = jnp.where(later >= earlier, raw, 0.0)
    upper = jnp.where(later <= earlier, 1.0, 0.0).astype(F32)
    summed[...] = LOG2E * jnp.dot(
        step[...], upper, precision=lax.Precision.HIGHEST, preferred_element_type=F32
    )
    keep = length // spread
    place = (later % keep) * spread + later // keep
    pick[...] = jnp.where(earlier == place, 1.0, 0.0).astype(BF16)


def mix_kernel(
    heads, sc, x_own, x_oth, w_own, w_oth, step, scores, summed, pick, out, joint
):
    core, used = sc[0], sc[1]
    j = pl.program_id(0)
    half, both_width = x_own.shape
    columns = pl.ds(pl.multiple_of(j * both_width, both_width), both_width)
    x_two, rows_two = joined(core, used, x_own[...], x_oth[:, columns], joint)
    width = both_width // 2
    length = 2 * half
    dim = width // heads
    pair = 2 * dim
    first = lax.broadcasted_iota(jnp.int32, (length, pair), 1) < dim
    for q in range(2):
        x, rows = x_two[:, q * width : (q + 1) * width], rows_two[:, :width]
        w = jnp.where(core == q, w_own[j], w_oth[j])
        x_act = conv_silu(x, w[0:4], w[4:5], rows)
        at = pl.ds(pl.multiple_of(16 * j + 8 * q, 8), 8)
        rates = -jnp.exp(w[6:7])
        sums_here = summed[at]
        scaled = [sums_here[h : h + 1] * rates[:, h * dim : h * dim + 1] for h in range(heads)]
        decay_rows = jnp.concatenate(scaled + [sums_here[heads:]], axis=0)
        decay_cols = jnp.transpose(decay_rows)
        step_cols = jnp.transpose(step[at])
        mixed = []
        for p in range(heads // 2):
            steps = jnp.where(
                first, step_cols[:, 2 * p : 2 * p + 1], step_cols[:, 2 * p + 1 : 2 * p + 2]
            )
            fed = x_act[:, p * pair : (p + 1) * pair] * steps
            fed_hi = fed.astype(BF16)
            fed_lo = (fed - fed_hi.astype(F32)).astype(BF16)
            fed_both = jnp.concatenate([fed_hi, fed_lo], axis=1)
            sums = []
            for h in (2 * p, 2 * p + 1):
                parts = []
                for lo, hi in ((0, half), (half, length)):
                    gap = decay_cols[lo:hi, h : h + 1] - decay_rows[h : h + 1, :hi]
                    weight = scores[lo:hi, :hi] * jnp.exp2(jnp.minimum(gap, 0.0))
                    both = jnp.dot(
                        weight.astype(BF16), fed_both[:hi], preferred_element_type=F32
                    )
                    parts.append(both[:, :pair] + both[:, pair:])
                sums.append(jnp.concatenate(parts, axis=0))
            mixed.append(jnp.where(first, sums[0], sums[1]))
        result = jnp.concatenate(mixed, axis=1) + w[5:6] * x_act
        out[q] = jnp.dot(
            pick[...], result.astype(BF16), preferred_element_type=F32
        ).astype(BF16)


def one_hot(size, place):
    at = lax.broadcasted_iota(jnp.int32, (size, place.shape[1]), 0)
    return jnp.where(at == place, 1.0, 0.0).astype(BF16)


def one_hot_back(size, place):
    count = place.shape[1]
    column = jnp.transpose(jnp.broadcast_to(place.astype(F32), (8, count)))[:, :1]
    at = lax.broadcasted_iota(jnp.int32, (count, size), 1).astype(F32)
    return jnp.where(at == column, 1.0, 0.0).astype(BF16)


def chosen(pick, rows):
    return jnp.dot(pick, rows, preferred_element_type=F32).astype(BF16)


def loop(count, body):
    def step(i, carry):
        body(i)
        return carry

    lax.fori_loop(0, count, step, 0, unroll=2)


def pack_kernel(sc, rows, place, out):
    pick = one_hot(out.shape[1], place[sc[0]])

    def body(i):
        out[i] = chosen(pick, rows[:, i].reshape(place.shape[2], rows.shape[3]))

    loop(out.shape[0], body)


def widen_kernel(rows, place, out):
    def body(i):
        one = chosen(one_hot_back(rows.shape[1], place[i]), rows[i])
        out[i] = one.reshape(out.shape[1:])

    loop(out.shape[0], body)


def order_kernel(count, source, rows, place, out):
    def body(z):
        blocks = []
        for g in range(count):
            i = source[z * count + g]
            blocks.append(rows[i // count, i % count])
        out[z] = chosen(one_hot(out.shape[1], place[z]), jnp.concatenate(blocks, axis=0))

    loop(out.shape[0], body)


def unpack_kernel(sc, rows, place, out):
    pick = one_hot_back(rows.shape[1], place[sc[0]])

    def body(i):
        one = chosen(pick, rows[i])
        out[:, i] = one.reshape((out.shape[0],) + out.shape[2:])

    loop(rows.shape[0], body)


def finish_kernel(spread, sc, rows, own, oth):
    core, last, filled = sc[0], sc[1], sc[2]
    length, width = rows.shape[1:]
    half = length // 2
    keep = length // spread
    source = lax.broadcasted_iota(jnp.int32, (length, length), 1)
    index = lax.broadcasted_iota(jnp.int32, (length, length), 0)
    swapped = jnp.where(index < half, index + half, index - half)
    t = jnp.minimum(jnp.where(core == 0, index, swapped), last)
    place = (t % spread) * keep + t // spread
    pick = jnp.where((source == place) & (filled > 0), 1.0, 0.0).astype(BF16)

    def body(j):
        picked = chosen(pick, rows[j])
        at = pl.ds(pl.multiple_of(j * width, width), width)
        own[:, at] = picked[:half]
        oth[:, at] = picked[half:]

    loop(rows.shape[0], body)


def norm_kernel(sc, own, oth, gain, out):
    core = sc[0]
    width = own.shape[1]
    count = out.shape[0]
    here = pl.ds(pl.multiple_of(pl.program_id(0) * count, count), count)
    mine, other = own[here].astype(F32), oth[here].astype(F32)
    total = jnp.sum(mine * mine, axis=1, keepdims=True) + jnp.sum(
        other * other, axis=1, keepdims=True
    )
    scale = lax.rsqrt(total / (2 * width) + 1e-05)
    for values, side in ((mine, core), (other, 1 - core)):
        at = pl.ds(pl.multiple_of(side * width, width), width)
        out[:, at] = (values * scale * gain[:, at]).astype(BF16)


def grid_spec(scalars, grid, ins, outs, scratch=()):
    return pltpu.PrefetchScalarGridSpec(
        num_scalar_prefetch=scalars,
        grid=grid,
        in_specs=ins,
        out_specs=outs,
        scratch_shapes=list(scratch),
    )


def resident():
    return pl.BlockSpec(memory_space=pltpu.VMEM)


def limits():
    return pltpu.CompilerParams(vmem_limit_bytes=24 << 20)


def once(kernel, scalars, outs, *operands, scratch=(), params=None):
    return pl.pallas_call(
        kernel,
        out_shape=outs,
        in_specs=[pl.BlockSpec(memory_space=pltpu.SMEM)] * scalars
        + [resident()] * (len(operands) - scalars),
        out_specs=jax.tree.map(lambda _: resident(), outs),
        scratch_shapes=list(scratch),
        compiler_params=params or limits(),
    )(*operands)


def per_device(
    x_in,
    bc_in,
    dt_in,
    dt_bias,
    a_log,
    skip_d,
    conv_x,
    conv_x_bias,
    conv_bc,
    conv_bc_bias,
    norm_gain,
    lengths,
    dest_group,
    dest_slot,
):
    n_ch = lax.axis_size("ch")
    n_grp = lax.axis_size("grp")
    n_z = n_ch // 2
    me = lax.axis_index("ch")
    my_group = lax.axis_index("grp")
    my_z, core = me // 2, me % 2
    half, channels = x_in.shape
    length = 2 * half
    mine = channels // 2
    width = channels // n_ch
    heads = a_log.shape[0]
    head_dim = width // heads
    head_half = dt_in.shape[1] // 2
    chunks = mine // width
    keep = length // n_z
    swap = [(i, i ^ 1) for i in range(n_ch)]
    rings = [[2 * z + c for z in range(n_z)] for c in range(2)]

    other_half = 1 - core
    shares = once(
        small_kernel,
        2,
        jax.ShapeDtypeStruct((n_z, 8, width), F32),
        skip_d,
        a_log,
        conv_x,
        conv_x_bias[None],
        params=pltpu.CompilerParams(),
    )

    shares, x_sent, bc_sent, dt_sent = lax.optimization_barrier((shares, x_in, bc_in, dt_in))
    x_oth = lax.ppermute(
        lax.dynamic_slice_in_dim(x_sent, other_half * mine, mine, 1), "ch", swap
    )
    bc_oth = lax.ppermute(bc_sent, "ch", swap)
    dt_oth = lax.ppermute(
        lax.dynamic_slice_in_dim(dt_sent, other_half * head_half, head_half, 1), "ch", swap
    )
    def exchange(a):
        return lax.all_to_all(
            a, "ch", split_axis=0, concat_axis=0, axis_index_groups=rings, tiled=True
        )

    by_chip = exchange(shares)
    pairs = n_grp * n_z
    ids = jnp.arange(pairs, dtype=jnp.int32)
    alive = dest_group >= 0
    units = jnp.where(alive, (jnp.minimum(lengths + 4, length) + n_z - 1) // n_z, 0)
    by_group = units.reshape(n_grp, n_z)
    ends = jnp.cumsum(by_group, axis=0)
    starts = ends - by_group
    target = jnp.where(alive, dest_group * n_z + dest_slot, pairs)
    match = target[None, :] == ids[:, None]

    def looked_up(values):
        return jnp.sum(jnp.where(match, values[None, :], 0), axis=1)

    to_units = looked_up(units).reshape(n_grp, n_z)
    slot_len = looked_up(lengths)
    source = looked_up((ids % n_z) * n_grp + ids // n_z)
    to_ends = jnp.cumsum(to_units, axis=0)
    to_starts = to_ends - to_units

    def places(count, start):
        k = jnp.arange(keep, dtype=jnp.int32)
        at = jnp.where(k < count.T[:, :, None], start.T[:, :, None] + k, -1)
        return at.reshape(n_z, 1, n_grp * keep)

    place_from = places(by_group, starts)
    place_to = places(to_units, to_starts)
    source = source.reshape(n_grp, n_z).T.reshape(-1)
    place_from, place_to, source = lax.optimization_barrier((place_from, place_to, source))
    z_only = my_z[None].astype(jnp.int32)

    my_dt = lax.dynamic_slice_in_dim(dt_in, core * head_half, head_half, 1)
    dt_both = jnp.concatenate(
        [jnp.where(core == 0, my_dt, dt_oth), jnp.where(core == 0, dt_oth, my_dt)], axis=0
    )
    used = lengths[my_group * n_z + my_z]
    valid = jnp.arange(length, dtype=jnp.int32) < used
    bias = lax.dynamic_slice_in_dim(dt_bias, core * head_half, head_half, 0)
    step = (
        jax.nn.softplus(dt_both.astype(F32) + bias[None, :]) * valid[:, None].astype(F32)
    ).astype(BF16).astype(F32)

    def by_chunk(a):
        a = a.reshape(chunks, heads, length)
        return jnp.pad(a, ((0, 0), (0, 8 - heads), (0, 0))).reshape(chunks * 8, length)

    step_t = by_chunk(step.T)
    wbc = jnp.concatenate([conv_bc, conv_bc_bias[None], jnp.zeros((3, conv_bc.shape[1]), F32)], axis=0)

    where_am_i = jnp.stack([core, used]).astype(jnp.int32)
    scores, summed, pick = once(
        functools.partial(prep_kernel, n_z),
        1,
        [
            jax.ShapeDtypeStruct((length, length), F32),
            jax.ShapeDtypeStruct(step_t.shape, F32),
            jax.ShapeDtypeStruct((length, length), BF16),
        ],
        where_am_i,
        bc_in,
        bc_oth,
        wbc,
        step_t,
        scratch=[pltpu.VMEM((2,) + bc_in.shape, BF16)],
        params=pltpu.CompilerParams(),
    )
    by_chip, scores = lax.optimization_barrier((by_chip, scores))
    n_half = n_z // 2
    w_own = lax.dynamic_slice_in_dim(by_chip, core * n_half, n_half, 0)
    w_oth = lax.ppermute(
        lax.dynamic_slice_in_dim(by_chip, other_half * n_half, n_half, 0), "ch", swap
    )
    mixed = pl.pallas_call(
        functools.partial(mix_kernel, heads),
        out_shape=jax.ShapeDtypeStruct((chunks, length, width), BF16),
        grid_spec=grid_spec(
            1,
            (chunks // 2,),
            [pl.BlockSpec((half, 2 * width), lambda j, sc: (0, sc[0] * (chunks // 2) + j))]
            + [resident()] * 7,
            pl.BlockSpec((2, length, width), lambda j, sc: (j, 0, 0)),
            [pltpu.VMEM((2, half, 2 * width), BF16)],
        ),
        name="mix",
    )(where_am_i, x_in, x_oth, w_own, w_oth, step_t, scores, summed, pick)

    spread = lax.all_to_all(mixed, "grp", split_axis=0, concat_axis=0, tiled=True)

    full = n_grp * keep
    by_pair = (n_grp, n_z, keep, width)
    wide_shape = (n_z, n_grp, keep, width)

    def bf16(*shape):
        return jax.ShapeDtypeStruct(shape, BF16)

    def outward(size, spread):
        outgoing = once(
            pack_kernel, 1, bf16(n_z, size, width), z_only, spread.reshape(by_pair), place_from
        )
        return once(widen_kernel, 0, bf16(*wide_shape), exchange(outgoing), place_from)

    def homeward(size, wide):
        ordered = once(
            functools.partial(order_kernel, n_grp), 1, bf16(n_z, size, width), source, wide, place_to
        )
        landed = once(unpack_kernel, 1, bf16(*by_pair), z_only, exchange(ordered), place_to)
        return landed.reshape(n_grp, length, width)

    sizes = [s for s in LEVELS if s < full] + [full]

    def sized(step, needed, rows):
        level = jnp.sum((jnp.max(needed) > jnp.array(sizes[:-1], jnp.int32)).astype(jnp.int32))
        return lax.switch(level, [functools.partial(step, s) for s in sizes], rows)

    wide = sized(outward, ends[-1], spread)
    landed = sized(homeward, to_ends[-1], wide)
    rows = lax.all_to_all(landed, "grp", split_axis=0, concat_axis=0, tiled=True)

    slot = my_group * n_z + my_z
    last = jnp.minimum(slot_len[slot] + 3, length - 1)
    filled = jnp.any(target == slot)
    ends_at = jnp.stack([core, last, filled.astype(jnp.int32)]).astype(jnp.int32)
    own, oth = once(
        functools.partial(finish_kernel, n_z), 1, [bf16(half, mine)] * 2, ends_at, rows
    )
    got = lax.ppermute(oth, "ch", swap)
    step_rows = 32
    return pl.pallas_call(
        norm_kernel,
        out_shape=jax.ShapeDtypeStruct((half, channels), BF16),
        grid_spec=grid_spec(
            1,
            (half // step_rows,),
            [resident()] * 3,
            pl.BlockSpec((step_rows, channels), lambda i, sc: (i, 0)),
        ),
        compiler_params=limits(),
        name="norm",
    )(ends_at, own, got, norm_gain[None])


def solution(mesh):
    placed = (
        P(("grp", "ch"), None),
        P(("grp", "ch"), None),
        P(("grp", "ch"), None),
        P(),
        P("ch"),
        P("ch"),
        P(None, "ch"),
        P("ch"),
        P(),
        P(),
        P(),
        P(),
        P(),
        P(),
    )
    return jax.shard_map(
        per_device, mesh=mesh, in_specs=placed, out_specs=P(("grp", "ch"), None), check_vma=False
    )
```

```python
import functools

import jax
import jax.numpy as jnp
from jax import lax
from jax.experimental import pallas as pl
from jax.experimental.pallas import tpu as pltpu
from jax.sharding import PartitionSpec as P

LEVELS = (128, 152, 160, 168, 176, 184, 192, 200, 216)
LOG2E = 1.4426950408889634
F32 = jnp.float32
BF16 = jnp.bfloat16


def conv_silu(values, taps, bias, rows):
    count = 4
    total = jnp.broadcast_to(bias, values.shape)
    for k in range(count):
        back = count - 1 - k
        moved = values
        if back:
            moved = pltpu.roll(values, back, 0)
            top = jnp.where(rows[:8] >= back, moved[:8], 0.0)
            moved = jnp.concatenate([top, moved[8:]], axis=0)
        total = total + taps[k : k + 1] * moved
    low = 0.5 * total
    return low + low * jnp.tanh(low)


def small_kernel(skip, rate, taps, bias, out):
    count, width = out.shape[0], out.shape[2]
    heads = skip.shape[0]
    lane = lax.broadcasted_iota(jnp.int32, (1, width), 1)

    def by_channel(values):
        spread = jnp.full((1, width), values[0], F32)
        for h in range(1, heads):
            spread = jnp.where(lane >= h * (width // heads), values[h], spread)
        return spread

    rows = [taps[...], bias[...], by_channel(skip), by_channel(rate), jnp.zeros((1, width), F32)]
    share = jnp.concatenate(rows, axis=0)
    for i in range(count):
        out[i] = share


def joined(core, used, own, oth, buffer):
    buffer[core] = own
    buffer[1 - core] = oth
    both = buffer[...].reshape(2 * own.shape[0], own.shape[1]).astype(F32)
    rows = lax.broadcasted_iota(jnp.int32, both.shape, 0)
    return jnp.where(rows < used, both, 0.0), rows


def prep_kernel(spread, sc, bc_own, bc_oth, wbc, step, scores, summed, pick, buffer):
    bc, rows = joined(sc[0], sc[1], bc_own[...], bc_oth[...], buffer)
    length = bc.shape[0]
    act = conv_silu(bc, wbc[0:4], wbc[4:5], rows)
    state = act.shape[1] // 2
    later = lax.broadcasted_iota(jnp.int32, (length, length), 0)
    earlier = lax.broadcasted_iota(jnp.int32, (length, length), 1)
    raw = lax.dot_general(
        act[:, state:],
        act[:, :state],
        (((1,), (1,)), ((), ())),
        precision=lax.Precision.HIGHEST,
        preferred_element_type=F32,
    )
    scores[...] = jnp.where(later >= earlier, raw, 0.0)
    upper = jnp.where(later <= earlier, 1.0, 0.0).astype(F32)
    summed[...] = LOG2E * jnp.dot(
        step[...], upper, precision=lax.Precision.HIGHEST, preferred_element_type=F32
    )
    keep = length // spread
    place = (later % keep) * spread + later // keep
    pick[...] = jnp.where(earlier == place, 1.0, 0.0).astype(BF16)


def mix_kernel(
    heads, sc, x_own, x_oth, w_own, w_oth, step, scores, summed, pick, out, joint
):
    core, used = sc[0], sc[1]
    j = pl.program_id(0)
    half, both_width = x_own.shape
    columns = pl.ds(pl.multiple_of(j * both_width, both_width), both_width)
    x_two, rows_two = joined(core, used, x_own[...], x_oth[:, columns], joint)
    width = both_width // 2
    length = 2 * half
    dim = width // heads
    pair = 2 * dim
    first = lax.broadcasted_iota(jnp.int32, (length, pair), 1) < dim
    for q in range(2):
        x, rows = x_two[:, q * width : (q + 1) * width], rows_two[:, :width]
        w = jnp.where(core == q, w_own[j], w_oth[j])
        x_act = conv_silu(x, w[0:4], w[4:5], rows)
        at = pl.ds(pl.multiple_of(16 * j + 8 * q, 8), 8)
        rates = -jnp.exp(w[6:7])
        sums_here = summed[at]
        scaled = [sums_here[h : h + 1] * rates[:, h * dim : h * dim + 1] for h in range(heads)]
        decay_rows = jnp.concatenate(scaled + [sums_here[heads:]], axis=0)
        decay_cols = jnp.transpose(decay_rows)
        step_cols = jnp.transpose(step[at])
        mixed = []
        for p in range(heads // 2):
            steps = jnp.where(
                first, step_cols[:, 2 * p : 2 * p + 1], step_cols[:, 2 * p + 1 : 2 * p + 2]
            )
            fed = x_act[:, p * pair : (p + 1) * pair] * steps
            fed_hi = fed.astype(BF16)
            fed_lo = (fed - fed_hi.astype(F32)).astype(BF16)
            fed_both = jnp.concatenate([fed_hi, fed_lo], axis=1)
            sums = []
            for h in (2 * p, 2 * p + 1):
                parts = []
                for lo, hi in ((0, half), (half, length)):
                    gap = decay_cols[lo:hi, h : h + 1] - decay_rows[h : h + 1, :hi]
                    weight = scores[lo:hi, :hi] * jnp.exp2(jnp.minimum(gap, 0.0))
                    both = jnp.dot(
                        weight.astype(BF16), fed_both[:hi], preferred_element_type=F32
                    )
                    parts.append(both[:, :pair] + both[:, pair:])
                sums.append(jnp.concatenate(parts, axis=0))
            mixed.append(jnp.where(first, sums[0], sums[1]))
        result = jnp.concatenate(mixed, axis=1) + w[5:6] * x_act
        out[q] = jnp.dot(
            pick[...], result.astype(BF16), preferred_element_type=F32
        ).astype(BF16)


def one_hot(size, place):
    at = lax.broadcasted_iota(jnp.int32, (size, place.shape[1]), 0)
    return jnp.where(at == place, 1.0, 0.0).astype(BF16)


def one_hot_back(size, place):
    count = place.shape[1]
    column = jnp.transpose(jnp.broadcast_to(place.astype(F32), (8, count)))[:, :1]
    at = lax.broadcasted_iota(jnp.int32, (count, size), 1).astype(F32)
    return jnp.where(at == column, 1.0, 0.0).astype(BF16)


def chosen(pick, rows):
    return jnp.dot(pick, rows, preferred_element_type=F32).astype(BF16)


def loop(count, body):
    def step(i, carry):
        body(i)
        return carry

    lax.fori_loop(0, count, step, 0, unroll=2)


def pack_kernel(sc, rows, place, out):
    pick = one_hot(out.shape[1], place[sc[0]])

    def body(i):
        out[i] = chosen(pick, rows[:, i].reshape(place.shape[2], rows.shape[3]))

    loop(out.shape[0], body)


def widen_kernel(rows, place, out):
    def body(i):
        one = chosen(one_hot_back(rows.shape[1], place[i]), rows[i])
        out[i] = one.reshape(out.shape[1:])

    loop(out.shape[0], body)


def order_kernel(count, source, rows, place, out):
    def body(z):
        blocks = []
        for g in range(count):
            i = source[z * count + g]
            blocks.append(rows[i // count, i % count])
        out[z] = chosen(one_hot(out.shape[1], place[z]), jnp.concatenate(blocks, axis=0))

    loop(out.shape[0], body)


def unpack_kernel(sc, rows, place, out):
    pick = one_hot_back(rows.shape[1], place[sc[0]])

    def body(i):
        one = chosen(pick, rows[i])
        out[:, i] = one.reshape((out.shape[0],) + out.shape[2:])

    loop(rows.shape[0], body)


def finish_kernel(spread, sc, rows, out):
    start, last, filled = sc[0], sc[1], sc[2]
    length, width = rows.shape[1:]
    half = length // 2
    keep = length // spread
    source = lax.broadcasted_iota(jnp.int32, (half, length), 1)
    index = lax.broadcasted_iota(jnp.int32, (half, length), 0)
    t = jnp.minimum(index + start, last)
    place = (t % spread) * keep + t // spread
    pick = jnp.where((source == place) & (filled > 0), 1.0, 0.0).astype(BF16)

    def body(j):
        at = pl.ds(pl.multiple_of(j * width, width), width)
        out[:, at] = chosen(pick, rows[j])

    loop(rows.shape[0], body)


def norm_kernel(sc, own, oth, gain, out):
    core = sc[0]
    width = own.shape[1]
    count = out.shape[0]
    here = pl.ds(pl.multiple_of(pl.program_id(0) * count, count), count)
    mine, other = own[here].astype(F32), oth[here].astype(F32)
    total = jnp.sum(mine * mine, axis=1, keepdims=True) + jnp.sum(
        other * other, axis=1, keepdims=True
    )
    scale = lax.rsqrt(total / (2 * width) + 1e-05)
    for values, side in ((mine, core), (other, 1 - core)):
        at = pl.ds(pl.multiple_of(side * width, width), width)
        out[:, at] = (values * scale * gain[:, at]).astype(BF16)


def grid_spec(scalars, grid, ins, outs, scratch=()):
    return pltpu.PrefetchScalarGridSpec(
        num_scalar_prefetch=scalars,
        grid=grid,
        in_specs=ins,
        out_specs=outs,
        scratch_shapes=list(scratch),
    )


def resident():
    return pl.BlockSpec(memory_space=pltpu.VMEM)


def limits():
    return pltpu.CompilerParams(vmem_limit_bytes=24 << 20)


def once(kernel, scalars, outs, *operands, scratch=(), params=None):
    return pl.pallas_call(
        kernel,
        out_shape=outs,
        in_specs=[pl.BlockSpec(memory_space=pltpu.SMEM)] * scalars
        + [resident()] * (len(operands) - scalars),
        out_specs=jax.tree.map(lambda _: resident(), outs),
        scratch_shapes=list(scratch),
        compiler_params=params or limits(),
    )(*operands)


def per_device(
    x_in,
    bc_in,
    dt_in,
    dt_bias,
    a_log,
    skip_d,
    conv_x,
    conv_x_bias,
    conv_bc,
    conv_bc_bias,
    norm_gain,
    lengths,
    dest_group,
    dest_slot,
):
    n_ch = lax.axis_size("ch")
    n_grp = lax.axis_size("grp")
    n_z = n_ch // 2
    me = lax.axis_index("ch")
    my_group = lax.axis_index("grp")
    my_z, core = me // 2, me % 2
    half, channels = x_in.shape
    length = 2 * half
    mine = channels // 2
    width = channels // n_ch
    heads = a_log.shape[0]
    head_dim = width // heads
    head_half = dt_in.shape[1] // 2
    chunks = mine // width
    keep = length // n_z
    swap = [(i, i ^ 1) for i in range(n_ch)]
    rings = [[2 * z + c for z in range(n_z)] for c in range(2)]

    other_half = 1 - core
    shares = once(
        small_kernel,
        2,
        jax.ShapeDtypeStruct((n_z, 8, width), F32),
        skip_d,
        a_log,
        conv_x,
        conv_x_bias[None],
        params=pltpu.CompilerParams(),
    )

    shares, x_sent, bc_sent, dt_sent = lax.optimization_barrier((shares, x_in, bc_in, dt_in))
    x_oth = lax.ppermute(
        lax.dynamic_slice_in_dim(x_sent, other_half * mine, mine, 1), "ch", swap
    )
    bc_oth = lax.ppermute(bc_sent, "ch", swap)
    dt_oth = lax.ppermute(
        lax.dynamic_slice_in_dim(dt_sent, other_half * head_half, head_half, 1), "ch", swap
    )
    def exchange(a):
        return lax.all_to_all(
            a, "ch", split_axis=0, concat_axis=0, axis_index_groups=rings, tiled=True
        )

    by_chip = exchange(shares)
    pairs = n_grp * n_z
    ids = jnp.arange(pairs, dtype=jnp.int32)
    alive = dest_group >= 0
    units = jnp.where(alive, (jnp.minimum(lengths + 4, length) + n_z - 1) // n_z, 0)
    by_group = units.reshape(n_grp, n_z)
    ends = jnp.cumsum(by_group, axis=0)
    starts = ends - by_group
    target = jnp.where(alive, dest_group * n_z + dest_slot, pairs)
    match = target[None, :] == ids[:, None]

    def looked_up(values):
        return jnp.sum(jnp.where(match, values[None, :], 0), axis=1)

    to_units = looked_up(units).reshape(n_grp, n_z)
    slot_len = looked_up(lengths)
    source = looked_up((ids % n_z) * n_grp + ids // n_z)
    to_ends = jnp.cumsum(to_units, axis=0)
    to_starts = to_ends - to_units

    def places(count, start):
        k = jnp.arange(keep, dtype=jnp.int32)
        at = jnp.where(k < count.T[:, :, None], start.T[:, :, None] + k, -1)
        return at.reshape(n_z, 1, n_grp * keep)

    place_from = places(by_group, starts)
    place_to = places(to_units, to_starts)
    source = source.reshape(n_grp, n_z).T.reshape(-1)
    place_from, place_to, source = lax.optimization_barrier((place_from, place_to, source))
    z_only = my_z[None].astype(jnp.int32)

    my_dt = lax.dynamic_slice_in_dim(dt_in, core * head_half, head_half, 1)
    dt_both = jnp.concatenate(
        [jnp.where(core == 0, my_dt, dt_oth), jnp.where(core == 0, dt_oth, my_dt)], axis=0
    )
    used = lengths[my_group * n_z + my_z]
    valid = jnp.arange(length, dtype=jnp.int32) < used
    bias = lax.dynamic_slice_in_dim(dt_bias, core * head_half, head_half, 0)
    step = (
        jax.nn.softplus(dt_both.astype(F32) + bias[None, :]) * valid[:, None].astype(F32)
    ).astype(BF16).astype(F32)

    def by_chunk(a):
        a = a.reshape(chunks, heads, length)
        return jnp.pad(a, ((0, 0), (0, 8 - heads), (0, 0))).reshape(chunks * 8, length)

    step_t = by_chunk(step.T)
    wbc = jnp.concatenate([conv_bc, conv_bc_bias[None], jnp.zeros((3, conv_bc.shape[1]), F32)], axis=0)

    where_am_i = jnp.stack([core, used]).astype(jnp.int32)
    scores, summed, pick = once(
        functools.partial(prep_kernel, n_z),
        1,
        [
            jax.ShapeDtypeStruct((length, length), F32),
            jax.ShapeDtypeStruct(step_t.shape, F32),
            jax.ShapeDtypeStruct((length, length), BF16),
        ],
        where_am_i,
        bc_in,
        bc_oth,
        wbc,
        step_t,
        scratch=[pltpu.VMEM((2,) + bc_in.shape, BF16)],
        params=pltpu.CompilerParams(),
    )
    by_chip, scores = lax.optimization_barrier((by_chip, scores))
    n_half = n_z // 2
    w_own = lax.dynamic_slice_in_dim(by_chip, core * n_half, n_half, 0)
    w_oth = lax.ppermute(
        lax.dynamic_slice_in_dim(by_chip, other_half * n_half, n_half, 0), "ch", swap
    )
    mixed = pl.pallas_call(
        functools.partial(mix_kernel, heads),
        out_shape=jax.ShapeDtypeStruct((chunks, length, width), BF16),
        grid_spec=grid_spec(
            1,
            (chunks // 2,),
            [pl.BlockSpec((half, 2 * width), lambda j, sc: (0, sc[0] * (chunks // 2) + j))]
            + [resident()] * 7,
            pl.BlockSpec((2, length, width), lambda j, sc: (j, 0, 0)),
            [pltpu.VMEM((2, half, 2 * width), BF16)],
        ),
        name="mix",
    )(where_am_i, x_in, x_oth, w_own, w_oth, step_t, scores, summed, pick)

    spread = lax.all_to_all(mixed, "grp", split_axis=0, concat_axis=0, tiled=True)

    full = n_grp * keep
    by_pair = (n_grp, n_z, keep, width)
    wide_shape = (n_z, n_grp, keep, width)

    def bf16(*shape):
        return jax.ShapeDtypeStruct(shape, BF16)

    def outward(size, spread):
        outgoing = once(
            pack_kernel, 1, bf16(n_z, size, width), z_only, spread.reshape(by_pair), place_from
        )
        return once(widen_kernel, 0, bf16(*wide_shape), exchange(outgoing), place_from)

    def homeward(size, wide):
        ordered = once(
            functools.partial(order_kernel, n_grp), 1, bf16(n_z, size, width), source, wide, place_to
        )
        landed = once(unpack_kernel, 1, bf16(*by_pair), z_only, exchange(ordered), place_to)
        return landed.reshape(n_grp, length, width)

    sizes = [s for s in LEVELS if s < full] + [full]

    def sized(step, needed, rows):
        level = jnp.sum((jnp.max(needed) > jnp.array(sizes[:-1], jnp.int32)).astype(jnp.int32))
        return lax.switch(level, [functools.partial(step, s) for s in sizes], rows)

    wide = sized(outward, ends[-1], spread)
    landed = sized(homeward, to_ends[-1], wide)
    rows = lax.all_to_all(landed, "grp", split_axis=0, concat_axis=0, tiled=True)

    slot = my_group * n_z + my_z
    last = jnp.minimum(slot_len[slot] + 3, length - 1)
    filled = jnp.any(target == slot)
    ends_at = jnp.stack([core, last, filled.astype(jnp.int32)]).astype(jnp.int32)
    tail = jnp.stack([last, filled.astype(jnp.int32)]).astype(jnp.int32)

    def finish(side):
        begins = jnp.concatenate([(side * half)[None].astype(jnp.int32), tail])
        return once(
            functools.partial(finish_kernel, n_z), 1, bf16(half, mine), begins, rows
        )

    oth = finish(1 - core)
    own = finish(core)
    got = lax.ppermute(oth, "ch", swap)
    step_rows = 32
    return pl.pallas_call(
        norm_kernel,
        out_shape=jax.ShapeDtypeStruct((half, channels), BF16),
        grid_spec=grid_spec(
            1,
            (half // step_rows,),
            [resident()] * 3,
            pl.BlockSpec((step_rows, channels), lambda i, sc: (i, 0)),
        ),
        compiler_params=limits(),
        name="norm",
    )(ends_at, own, got, norm_gain[None])


def solution(mesh):
    placed = (
        P(("grp", "ch"), None),
        P(("grp", "ch"), None),
        P(("grp", "ch"), None),
        P(),
        P("ch"),
        P("ch"),
        P(None, "ch"),
        P("ch"),
        P(),
        P(),
        P(),
        P(),
        P(),
        P(),
    )
    return jax.shard_map(
        per_device, mesh=mesh, in_specs=placed, out_specs=P(("grp", "ch"), None), check_vma=False
    )
```
